32 devices in a mesh: pair: 16 (over z, y, x), dp: 2 (over core).
Axes of the slice: x: 2, y: 2, z: 4, core: 2. Of those that a mesh axis runs over, the one named last changes fastest.
Arguments:
- features: bfloat16 [16384, 2048], P(('pair', 'dp')), may hold values from -6 to 6
- proj_weight: bfloat16 [2048, 128], replicated, may hold values from -0.01171875 to 0.01171875
- row_lse: bfloat16 [16384], P(('pair', 'dp')), may hold values from 6 to 9
- positive: int32 [16384], P(('pair', 'dp')), may hold values from 0 to 16383, as said below
Outputs:
- grad_embed: float32 [16384, 128], P(('pair', 'dp'))
- grad_weight: float32 [2048, 128], P('dp')
The draws below stay inside these ranges and needn't reach their ends.
Inputs may be any that keep to these rules, and one draw needn't show every extreme that they name: positive[i] names the row that holds the other view of row i's cutout: positive[positive[i]] = i and positive[i] != i.
All inputs are finite; a program needn't handle non-finite values.
Results may differ from the reference program's by a relative error of at most 0.0045.
Values may be sent and summed in bfloat16 or wider, within the bound.
No kernel may reach another device: no remote copies, remote signals or barrier semaphores. Data moves between devices by JAX's collectives and lax.ppermute only.
A program may use at most 64 MiB of HBM per device.

```python
import jax
import jax.numpy as jnp
from jax import lax

F = 2048
P_SIZE = 128
GROUP = 1024
ROWS = 16384
N_PAIR = 16


def draw_positive(key, part):
    shuffled = jax.random.permutation(key, ROWS).astype(jnp.int32)
    couples = shuffled.reshape(-1, 2)
    swapped = couples[:, ::-1].reshape(-1)
    return jnp.zeros((ROWS,), jnp.int32).at[shuffled].set(swapped)


def block_levels(stream_key, extent, split, smallest, largest):
    loudness, own = 1.0, jax.random.fold_in(stream_key, 6)
    for dim, parts in split:
        draws = jnp.exp(jax.random.uniform(jax.random.fold_in(own, dim), (parts,), jnp.float32, smallest / len(split), largest / len(split)))
        loudness = loudness * jnp.repeat(draws, extent[dim] // parts).reshape([-1 if axis == dim else 1 for axis in range(len(extent))])
    return loudness


def bell_draw(rng, shape, scale, most, shards=(), kind=jnp.bfloat16):
    loudness = block_levels(rng, shape, shards, -0.22, 0.18) if shards else 1.0
    array = jax.random.normal(rng, shape, jnp.float32) * scale * loudness
    return jnp.minimum(jnp.maximum(array, -most), most).astype(kind)


def setup_inputs(seed: int = 0) -> dict:
    seeds = jax.random.split(jax.random.key(seed), 5)
    features = bell_draw(seeds[0], (ROWS, F), 1.0, 6.0, ((0, 32),))
    proj_weight = bell_draw(seeds[1], (F, P_SIZE), (F * P_SIZE) ** -0.5, 0.01171875)
    row_lse = jnp.clip(6.0 + 3.0 * jax.random.uniform(seeds[2], (ROWS,), jnp.float32) ** block_levels(seeds[2], (ROWS,), ((0, 32),), -0.2, 0.2), 6.0, 9.0).astype(jnp.bfloat16)
    positive = draw_positive(jax.random.fold_in(seeds[4], 71), 0)
    return {"features": features, "proj_weight": proj_weight, "row_lse": row_lse, "positive": positive}


contrastive_divisor = 0.1
epsilon = 1e-06

def couple(resident_feature_vectors, own_lse, own_positive, counterpart_feature_vectors, part_lse, first_id):
    cosine_affinity_matrix = jnp.dot(resident_feature_vectors, counterpart_feature_vectors.T, preferred_element_type=jnp.float32) / contrastive_divisor
    weights = jnp.exp(cosine_affinity_matrix - own_lse.astype(jnp.float32)[:, None]) + jnp.exp(cosine_affinity_matrix - part_lse.astype(jnp.float32)[None, :])
    identity_rows = first_id + jnp.arange(counterpart_feature_vectors.shape[0], dtype=jnp.int32)
    matched = (own_positive[:, None] == identity_rows[None, :]).astype(jnp.float32)
    return (weights - 2.0 * matched).astype(jnp.bfloat16)

def reference(features, proj_weight, row_lse, positive):
    far_offset = N_PAIR // 4
    projected = jnp.dot(features, proj_weight, preferred_element_type=jnp.float32)
    magnitude = jnp.sqrt(lax.optimization_barrier(jnp.sum(projected * projected, axis=-1, keepdims=True)) + epsilon)
    unit = projected / magnitude
    embedded = unit.astype(jnp.bfloat16)
    embed_blocks = embedded.reshape(N_PAIR, GROUP, P_SIZE)
    lse_blocks = row_lse.reshape(N_PAIR, GROUP)
    positive_blocks = positive.reshape(N_PAIR, GROUP)

    def one_block(block_id):
        resident_feature_vectors = embed_blocks[block_id]
        upstream_derivative = jnp.zeros((GROUP, P_SIZE), jnp.float32)
        for signed_offset in (1, -1, far_offset, -far_offset):
            partner = jnp.remainder(block_id - signed_offset, N_PAIR).astype(jnp.int32)
            counterpart_feature_vectors = embed_blocks[partner]
            coupling = couple(resident_feature_vectors, lse_blocks[block_id], positive_blocks[block_id], counterpart_feature_vectors, lse_blocks[partner], (partner * GROUP).astype(jnp.int32))
            upstream_derivative = upstream_derivative + jnp.dot(coupling, counterpart_feature_vectors, preferred_element_type=jnp.float32)
        return upstream_derivative
    gathered_feature_matrix = lax.map(one_block, jnp.arange(N_PAIR, dtype=jnp.int32)).reshape(ROWS, P_SIZE)
    derivative_pair_affinity = gathered_feature_matrix / contrastive_divisor
    grad_embed = (derivative_pair_affinity - unit * lax.optimization_barrier(jnp.sum(unit * derivative_pair_affinity, axis=-1, keepdims=True))) / magnitude
    grad_half = grad_embed.astype(jnp.bfloat16)
    grad_weight = jnp.dot(features.T, grad_half, preferred_element_type=jnp.float32)
    return (grad_embed, grad_weight)
```

```python
import functools
import math

import jax
import jax.numpy as jnp
from jax import lax
from jax.experimental import pallas as pl
from jax.experimental.pallas import tpu as pltpu
from jax.sharding import PartitionSpec as P

inverse_temperature = 10.0
exponent_scale = 10.0 * math.log2(math.e)
epsilon = 1e-06
lanes = 128
tail = 16
f32, bf16 = jnp.float32, jnp.bfloat16


def shifted(value, axis, steps):
    count = lax.axis_size(axis)
    return lax.ppermute(value, axis, [(s, (s + steps) % count) for s in range(count)])


def swapped(value, axis, mask):
    count = lax.axis_size(axis)
    return lax.ppermute(value, axis, [(s, s ^ mask) for s in range(count)])


def vmem_spec():
    return pl.BlockSpec(memory_space=pltpu.VMEM)


def smem_spec():
    return pl.BlockSpec(memory_space=pltpu.SMEM)


def project_kernel(features_ref, weight_ref, lse_ref, projected_ref, packed_ref):
    step = pl.program_id(0)
    chunk = features_ref.shape[0]
    rows = pl.ds(pl.multiple_of(step * chunk, chunk), chunk)
    projected = jnp.dot(features_ref[...], weight_ref[...], preferred_element_type=f32)
    magnitude = jnp.sqrt(jnp.sum(projected * projected, axis=-1, keepdims=True) + epsilon)
    projected_ref[rows, :] = projected
    packed_ref[rows, :] = (projected / magnitude).astype(bf16)

    @pl.when(step == 0)
    def _():
        count = packed_ref.shape[0] - tail
        packed_ref[pl.ds(count, tail), :] = lse_ref[...]


def project(features, weight, lse_rows):
    rows, units = features.shape
    width = weight.shape[1]
    chunk = min(128, rows)
    return pl.pallas_call(
        project_kernel,
        grid=(rows // chunk,),
        in_specs=[
            pl.BlockSpec((chunk, units), lambda i: (i, 0)),
            pl.BlockSpec((units, width), lambda i: (0, 0)),
            pl.BlockSpec((tail, lanes), lambda i: (0, 0)),
        ],
        out_specs=[
            pl.BlockSpec((rows, width), lambda i: (0, 0)),
            pl.BlockSpec((rows + tail, width), lambda i: (0, 0)),
        ],
        out_shape=[
            jax.ShapeDtypeStruct((rows, width), f32),
            jax.ShapeDtypeStruct((rows + tail, width), bf16),
        ],
        compiler_params=pltpu.CompilerParams(vmem_limit_bytes=32 * 2**20),
        name="project",
    )(features, weight, lse_rows)


def as_columns(rows):
    return jnp.concatenate(
        [
            jnp.broadcast_to(rows[k : k + 1, :], (lanes, lanes)).T
            for k in range(rows.shape[0])
        ],
        axis=0,
    )


def couple_kernel(count, first, base_ref, own_ref, positive_ref, *refs):
    parts = refs[:count]
    acc_ref = refs[count + (0 if first else 1)]
    rows = own_ref.shape[0] - tail
    chunk = min(256, rows)
    own_weight = as_columns(jnp.exp(-own_ref[pl.ds(rows, tail), :].astype(f32))[: rows // lanes, :])
    own_positive = as_columns(positive_ref[...].astype(f32))
    column = lax.broadcasted_iota(jnp.int32, (1, lanes), 1)
    for start in range(0, rows, chunk):
        own = own_ref[pl.ds(start, chunk), :]
        weight_i = own_weight[start : start + chunk, :]
        positive_i = own_positive[start : start + chunk, :]
        total = jnp.zeros((chunk, own.shape[1]), f32) if first else refs[count][pl.ds(start, chunk), :]
        for which, part in enumerate(parts):
            part_weight = jnp.exp(-part[pl.ds(rows, tail), :].astype(f32))
            for begin in range(0, rows, chunk):
                other = part[pl.ds(begin, chunk), :]
                cosine = lax.dot_general(
                    own, other, (((1,), (1,)), ((), ())), preferred_element_type=f32
                )
                pieces = []
                for lane in range(0, chunk, lanes):
                    k = (begin + lane) // lanes
                    grown = jnp.exp2(cosine[:, lane : lane + lanes] * exponent_scale)
                    ids = (column + (base_ref[which] + (begin + lane))).astype(f32)
                    value = grown * (weight_i + part_weight[k : k + 1, :])
                    value = value - jnp.where(positive_i == ids, 2.0, 0.0)
                    pieces.append(value.astype(bf16))
                coupling = jnp.concatenate(pieces, axis=1)
                total = total + jnp.dot(coupling, other, preferred_element_type=f32)
        acc_ref[pl.ds(start, chunk), :] = total


def couple(base, own, positive, parts, acc=None):
    rows = own.shape[0] - tail
    width = own.shape[1]
    count = len(parts)
    extra = [] if acc is None else [acc]
    pairs = rows * rows * count
    return pl.pallas_call(
        functools.partial(couple_kernel, count, acc is None),
        in_specs=[smem_spec()] + [vmem_spec()] * (2 + count + len(extra)),
        out_specs=vmem_spec(),
        out_shape=jax.ShapeDtypeStruct((rows, width), f32),
        compiler_params=pltpu.CompilerParams(vmem_limit_bytes=32 * 2**20),
        cost_estimate=pl.CostEstimate(
            flops=4 * pairs * width, bytes_accessed=rows * width * 4, transcendentals=pairs
        ),
        name="couple",
    )(base, own, positive, *parts, *extra)


def finish_kernel(acc_ref, projected_ref, grad_ref, half_ref):
    projected = projected_ref[...]
    magnitude = jnp.sqrt(jnp.sum(projected * projected, axis=-1, keepdims=True) + epsilon)
    unit = projected / magnitude
    upstream = acc_ref[...] * inverse_temperature
    grad = (upstream - unit * jnp.sum(unit * upstream, axis=-1, keepdims=True)) / magnitude
    grad_ref[...] = grad
    half_ref[...] = grad.astype(bf16)


def finish(acc, projected):
    return pl.pallas_call(
        finish_kernel,
        in_specs=[vmem_spec()] * 2,
        out_specs=[vmem_spec()] * 2,
        out_shape=[
            jax.ShapeDtypeStruct(projected.shape, f32),
            jax.ShapeDtypeStruct(projected.shape, bf16),
        ],
        name="finish",
    )(acc, projected)


def weight_kernel(which_ref, features_ref, half_ref, out_ref):
    out_ref[...] = lax.dot_general(
        features_ref[...], half_ref[...], (((0,), (0,)), ((), ())), preferred_element_type=f32
    ).astype(out_ref.dtype)


def weight_term(features, grad_half, share, shares, dtype):
    rows, units = features.shape
    width = grad_half.shape[1]
    size = units // shares
    chunk = min(256, size)
    per = size // chunk
    return pl.pallas_call(
        weight_kernel,
        grid_spec=pltpu.PrefetchScalarGridSpec(
            num_scalar_prefetch=1,
            grid=(per,),
            in_specs=[
                pl.BlockSpec((rows, chunk), lambda i, which: (0, which[0] * per + i)),
                pl.BlockSpec((rows, width), lambda i, which: (0, 0)),
            ],
            out_specs=pl.BlockSpec((chunk, width), lambda i, which: (i, 0)),
        ),
        out_shape=jax.ShapeDtypeStruct((size, width), dtype),
        cost_estimate=pl.CostEstimate(
            flops=2 * rows * size * width, bytes_accessed=rows * size * 2, transcendentals=0
        ),
        name="weight_term",
    )(share[None], features, grad_half)


def split_kernel(count, digit_ref, own_ref, *refs):
    parts, keep_ref, sends = refs[:count], refs[count], refs[count + 1 :]
    size = keep_ref.shape[0]
    for s in range(len(sends) + 1):
        rows = pl.ds(pl.multiple_of((digit_ref[0] ^ s) * size, size), size)
        total = own_ref[rows, :]
        for part in parts:
            total = total + part[rows, :].astype(f32)
        if s == 0:
            keep_ref[...] = total
        else:
            sends[s - 1][...] = total.astype(bf16)


def split(digit, own, parts, ways):
    size = own.shape[0] // ways
    return pl.pallas_call(
        functools.partial(split_kernel, len(parts)),
        in_specs=[smem_spec()] + [vmem_spec()] * (1 + len(parts)),
        out_specs=[vmem_spec()] * ways,
        out_shape=[jax.ShapeDtypeStruct((size, own.shape[1]), f32)]
        + [jax.ShapeDtypeStruct((size, own.shape[1]), bf16)] * (ways - 1),
        name="split",
    )(digit[None], own, *parts)


def join_kernel(digit_ref, *refs):
    parts, out_ref = refs[:-1], refs[-1]
    size = parts[0].shape[0]
    for s, part in enumerate(parts):
        rows = pl.ds(pl.multiple_of((digit_ref[0] ^ s) * size, size), size)
        out_ref[rows, :] = part[...].astype(f32)


def join(digit, parts):
    size, width = parts[0].shape
    return pl.pallas_call(
        join_kernel,
        in_specs=[smem_spec()] + [vmem_spec()] * len(parts),
        out_specs=vmem_spec(),
        out_shape=jax.ShapeDtypeStruct((size * len(parts), width), f32),
        name="join",
    )(digit[None], *parts)


def body(features, proj_weight, row_lse, positive):
    rows = features.shape[0]
    dp_count = lax.axis_size("dp")
    pair_count = lax.axis_size("pair")
    far = pair_count // 4
    group_rows = rows * dp_count
    block = lax.axis_index("pair").astype(jnp.int32)
    core = lax.axis_index("dp").astype(jnp.int32)

    lse_rows = jnp.pad(row_lse.reshape(rows // lanes, lanes), ((0, tail - rows // lanes), (0, 0)))
    positive_rows = positive.reshape(rows // lanes, lanes)
    projected, packed = project(features, proj_weight, lse_rows)

    bases, parts = [], []
    for offset in (1, -1, far, -far):
        part = shifted(packed, "pair", offset)
        first = jnp.remainder(block - offset, pair_count) * group_rows
        for mask in range(dp_count):
            parts.append(part if mask == 0 else swapped(part, "dp", mask))
            bases.append(first + (core ^ mask) * rows)
    acc = couple(jnp.stack(bases), packed, positive_rows, parts)
    grad_embed, grad_half = finish(acc, projected)

    received = [
        swapped(weight_term(features, grad_half, core ^ mask, dp_count, bf16), "dp", mask)
        for mask in range(1, dp_count)
    ]
    mine = weight_term(features, grad_half, core, dp_count, f32)

    ways = 4
    digit = block & (ways - 1)
    keep, *sends = split(digit, mine, received, ways)
    for s in range(1, ways):
        keep = keep + swapped(sends[s - 1], "pair", s).astype(f32)
    stride = ways
    while stride < pair_count:
        mine = keep.astype(bf16)
        near, middle, last = (swapped(mine, "pair", s * stride).astype(f32) for s in (1, 2, 3))
        keep = (mine.astype(f32) + near) + (middle + last)
        stride *= ways
    mine = keep.astype(bf16)
    quarters = [mine] + [swapped(mine, "pair", s) for s in range(1, ways)]
    return (grad_embed, join(digit, quarters))


def solution(mesh):
    return jax.shard_map(
        body,
        mesh=mesh,
        in_specs=(P(("pair", "dp"), None), P(), P(("pair", "dp")), P(("pair", "dp"))),
        out_specs=(P(("pair", "dp"), None), P("dp", None)),
        check_vma=False,
    )
```

```python
import functools
import math

import jax
import jax.numpy as jnp
from jax import lax
from jax.experimental import pallas as pl
from jax.experimental.pallas import tpu as pltpu
from jax.sharding import PartitionSpec as P

inverse_temperature = 10.0
exponent_scale = 10.0 * math.log2(math.e)
epsilon = 1e-06
lanes = 128
tail = 16
f32, bf16 = jnp.float32, jnp.bfloat16


def shifted(value, axis, steps):
    count = lax.axis_size(axis)
    return lax.ppermute(value, axis, [(s, (s + steps) % count) for s in range(count)])


def swapped(value, axis, mask):
    count = lax.axis_size(axis)
    return lax.ppermute(value, axis, [(s, s ^ mask) for s in range(count)])


def vmem_spec():
    return pl.BlockSpec(memory_space=pltpu.VMEM)


def smem_spec():
    return pl.BlockSpec(memory_space=pltpu.SMEM)


def small_grant(mib):
    return pltpu.CompilerParams(vmem_limit_bytes=mib * 2**20)


def project_kernel(
    features_ref, weight_ref, lse_ref, projected_ref, packed_ref, held, weight, weight_sem, sems
):
    rows = held.shape[0]
    chunk = rows // sems.shape[0]
    weight_copy = pltpu.make_async_copy(weight_ref, weight, weight_sem)
    weight_copy.start()
    copies = []
    for k in range(sems.shape[0]):
        part = pl.ds(k * chunk, chunk)
        copy = pltpu.make_async_copy(features_ref.at[part, :], held.at[part, :], sems.at[k])
        copy.start()
        copies.append(copy)
    packed_ref[pl.ds(rows, tail), :] = lse_ref[...]
    weight_copy.wait()
    for k, copy in enumerate(copies):
        part = pl.ds(k * chunk, chunk)
        copy.wait()
        projected = jnp.dot(held[part, :], weight[...], preferred_element_type=f32)
        magnitude = jnp.sqrt(jnp.sum(projected * projected, axis=-1, keepdims=True) + epsilon)
        projected_ref[part, :] = projected
        packed_ref[part, :] = (projected / magnitude).astype(bf16)


def project(features, weight, lse_rows):
    rows, units = features.shape
    width = weight.shape[1]
    chunks = 4
    hbm = pl.BlockSpec(memory_space=pltpu.HBM)
    return pl.pallas_call(
        project_kernel,
        in_specs=[hbm, hbm, vmem_spec()],
        out_specs=[vmem_spec()] * 2,
        out_shape=[
            jax.ShapeDtypeStruct((rows, width), f32),
            jax.ShapeDtypeStruct((rows + tail, width), bf16),
        ],
        scratch_shapes=[
            pltpu.VMEM((rows, units), bf16),
            pltpu.VMEM((units, width), bf16),
            pltpu.SemaphoreType.DMA,
            pltpu.SemaphoreType.DMA((chunks,)),
        ],
        compiler_params=small_grant(8),
        name="project",
    )(features, weight, lse_rows)


def as_columns(rows):
    return jnp.concatenate(
        [
            jnp.broadcast_to(rows[k : k + 1, :], (lanes, lanes)).T
            for k in range(rows.shape[0])
        ],
        axis=0,
    )


def coupled_rows(start, chunk, own_weight, own_positive, base_ref, own_ref, parts, total):
    rows = own_ref.shape[0] - tail
    column = lax.broadcasted_iota(jnp.int32, (1, lanes), 1)
    own = own_ref[pl.ds(start, chunk), :]
    weight_i = own_weight[start : start + chunk, :]
    positive_i = own_positive[start : start + chunk, :]
    for which, part in enumerate(parts):
        part_weight = jnp.exp(-part[pl.ds(rows, tail), :].astype(f32))
        for begin in range(0, rows, chunk):
            other = part[pl.ds(begin, chunk), :]
            cosine = lax.dot_general(
                own, other, (((1,), (1,)), ((), ())), preferred_element_type=f32
            )
            pieces = []
            for lane in range(0, chunk, lanes):
                k = (begin + lane) // lanes
                grown = jnp.exp2(cosine[:, lane : lane + lanes] * exponent_scale)
                ids = (column + (base_ref[which] + (begin + lane))).astype(f32)
                value = grown * (weight_i + part_weight[k : k + 1, :])
                value = value - jnp.where(positive_i == ids, 2.0, 0.0)
                pieces.append(value.astype(bf16))
            coupling = jnp.concatenate(pieces, axis=1)
            total = total + jnp.dot(coupling, other, preferred_element_type=f32)
    return total


def own_columns(own_ref, positive_ref):
    rows = own_ref.shape[0] - tail
    own_weight = as_columns(jnp.exp(-own_ref[pl.ds(rows, tail), :].astype(f32))[: rows // lanes, :])
    return own_weight, as_columns(positive_ref[...].astype(f32))


def couple_kernel(base_ref, own_ref, positive_ref, *refs):
    parts, acc_ref = refs[:-1], refs[-1]
    rows = own_ref.shape[0] - tail
    chunk = min(256, rows)
    columns = own_columns(own_ref, positive_ref)
    for start in range(0, rows, chunk):
        total = jnp.zeros((chunk, own_ref.shape[1]), f32)
        acc_ref[pl.ds(start, chunk), :] = coupled_rows(
            start, chunk, *columns, base_ref, own_ref, parts, total
        )


def couple_cost(rows, width, count):
    pairs = rows * rows * count
    return pl.CostEstimate(
        flops=4 * pairs * width, bytes_accessed=rows * width * 4, transcendentals=pairs
    )


def couple(base, own, positive, parts):
    rows, width = own.shape[0] - tail, own.shape[1]
    return pl.pallas_call(
        couple_kernel,
        in_specs=[smem_spec()] + [vmem_spec()] * (2 + len(parts)),
        out_specs=vmem_spec(),
        out_shape=jax.ShapeDtypeStruct((rows, width), f32),
        compiler_params=small_grant(8),
        cost_estimate=couple_cost(rows, width, len(parts)),
        name="couple",
    )(base, own, positive, *parts)


def finish_kernel(
    count, shares, base_ref, own_ref, positive_ref, acc_ref, projected_ref, features_ref, *refs
):
    parts, grad_ref, half_ref, sends = refs[:count], refs[count], refs[count + 1], refs[count + 2 :]
    rows = own_ref.shape[0] - tail
    chunk = min(256, rows)
    columns = own_columns(own_ref, positive_ref)
    for start in range(0, rows, chunk):
        part = pl.ds(start, chunk)
        total = coupled_rows(
            start, chunk, *columns, base_ref, own_ref, parts, acc_ref[part, :]
        )
        projected = projected_ref[part, :]
        magnitude = jnp.sqrt(jnp.sum(projected * projected, axis=-1, keepdims=True) + epsilon)
        unit = projected / magnitude
        upstream = total * inverse_temperature
        grad = (upstream - unit * jnp.sum(unit * upstream, axis=-1, keepdims=True)) / magnitude
        grad_ref[part, :] = grad
        half_ref[:, part] = grad.T.astype(bf16)
    for mask, send in enumerate(sends, 1):
        share = base_ref[count] ^ mask
        weight_columns(half_ref, features_ref, share, send)


def weight_columns(half_ref, features_ref, share, out_ref):
    size = out_ref.shape[1]
    chunk = min(256, size)
    for start in range(0, size, chunk):
        columns = pl.ds(pl.multiple_of(share * size + start, chunk), chunk)
        out_ref[:, pl.ds(start, chunk)] = jnp.dot(
            half_ref[...], features_ref[:, columns], preferred_element_type=f32
        ).astype(out_ref.dtype)


def finish(base, own, positive, acc, projected, features, parts, shares):
    rows, width = projected.shape
    units = features.shape[1]
    return pl.pallas_call(
        functools.partial(finish_kernel, len(parts), shares),
        in_specs=[smem_spec()] + [vmem_spec()] * (5 + len(parts)),
        out_specs=[vmem_spec()] * (1 + shares),
        out_shape=[
            jax.ShapeDtypeStruct((rows, width), f32),
            jax.ShapeDtypeStruct((width, rows), bf16),
        ]
        + [jax.ShapeDtypeStruct((width, units // shares), bf16)] * (shares - 1),
        compiler_params=small_grant(8),
        cost_estimate=couple_cost(rows, width, len(parts)),
        name="finish",
    )(base, own, positive, acc, projected, features, *parts)


def weight_kernel(share_ref, half_ref, features_ref, out_ref):
    weight_columns(half_ref, features_ref, share_ref[0], out_ref)


def weight_term(half, features, share, shares):
    width, rows = half.shape
    size = features.shape[1] // shares
    return pl.pallas_call(
        weight_kernel,
        in_specs=[smem_spec()] + [vmem_spec()] * 2,
        out_specs=vmem_spec(),
        out_shape=jax.ShapeDtypeStruct((width, size), f32),
        compiler_params=small_grant(8),
        cost_estimate=pl.CostEstimate(
            flops=2 * rows * size * width, bytes_accessed=rows * size * 2, transcendentals=0
        ),
        name="weight_term",
    )(share[None], half, features)


def split_kernel(count, digit_ref, own_ref, *refs):
    parts, keep_ref, sends = refs[:count], refs[count], refs[count + 1 :]
    size = keep_ref.shape[1]
    for s in range(len(sends) + 1):
        columns = pl.ds(pl.multiple_of((digit_ref[0] ^ s) * size, size), size)
        total = own_ref[:, columns]
        for part in parts:
            total = total + part[:, columns].astype(f32)
        if s == 0:
            keep_ref[...] = total
        else:
            sends[s - 1][...] = total.astype(bf16)


def split(digit, own, parts, ways):
    width, size = own.shape[0], own.shape[1] // ways
    return pl.pallas_call(
        functools.partial(split_kernel, len(parts)),
        in_specs=[smem_spec()] + [vmem_spec()] * (1 + len(parts)),
        out_specs=[vmem_spec()] * ways,
        out_shape=[jax.ShapeDtypeStruct((width, size), f32)]
        + [jax.ShapeDtypeStruct((width, size), bf16)] * (ways - 1),
        compiler_params=small_grant(4),
        name="split",
    )(digit[None], own, *parts)


def join_kernel(digit_ref, *refs):
    parts, out_ref = refs[:-1], refs[-1]
    size = parts[0].shape[1]
    for s, part in enumerate(parts):
        rows = pl.ds(pl.multiple_of((digit_ref[0] ^ s) * size, size), size)
        out_ref[rows, :] = part[...].astype(f32).T


def join(digit, parts):
    width, size = parts[0].shape
    return pl.pallas_call(
        join_kernel,
        in_specs=[smem_spec()] + [vmem_spec()] * len(parts),
        out_specs=vmem_spec(),
        out_shape=jax.ShapeDtypeStruct((size * len(parts), width), f32),
        compiler_params=small_grant(4),
        name="join",
    )(digit[None], *parts)


def body(features, proj_weight, row_lse, positive):
    rows = features.shape[0]
    dp_count = lax.axis_size("dp")
    pair_count = lax.axis_size("pair")
    far = pair_count // 4
    group_rows = rows * dp_count
    block = lax.axis_index("pair").astype(jnp.int32)
    core = lax.axis_index("dp").astype(jnp.int32)

    lse_rows = jnp.pad(row_lse.reshape(rows // lanes, lanes), ((0, tail - rows // lanes), (0, 0)))
    positive_rows = positive.reshape(rows // lanes, lanes)
    projected, packed = project(features, proj_weight, lse_rows)

    def partner(*offsets):
        bases, parts = [], []
        for offset in offsets:
            part = shifted(packed, "pair", offset)
            first = jnp.remainder(block - offset, pair_count) * group_rows
            for mask in range(dp_count):
                parts.append(part if mask == 0 else swapped(part, "dp", mask))
                bases.append(first + (core ^ mask) * rows)
        return jnp.stack(bases + [core]), parts

    far_bases, far_parts = partner(far, -far)
    near_bases, near_parts = partner(1, -1)
    acc = couple(far_bases, packed, positive_rows, far_parts)
    grad_embed, half, *sends = finish(
        near_bases, packed, positive_rows, acc, projected, features, near_parts, dp_count
    )
    received = [swapped(send, "dp", mask) for mask, send in enumerate(sends, 1)]
    mine = weight_term(half, features, core, dp_count)

    ways = 4
    digit = block & (ways - 1)
    keep, *sends = split(digit, mine, received, ways)
    for s in range(1, ways):
        keep = keep + swapped(sends[s - 1], "pair", s).astype(f32)
    stride = ways
    while stride < pair_count:
        mine = keep.astype(bf16)
        near, middle, last = (swapped(mine, "pair", s * stride).astype(f32) for s in (1, 2, 3))
        keep = (mine.astype(f32) + near) + (middle + last)
        stride *= ways
    mine = keep.astype(bf16)
    quarters = [mine] + [swapped(mine, "pair", s) for s in range(1, ways)]
    return (grad_embed, join(digit, quarters))


def solution(mesh):
    return jax.shard_map(
        body,
        mesh=mesh,
        in_specs=(P(("pair", "dp"), None), P(), P(("pair", "dp")), P(("pair", "dp"))),
        out_specs=(P(("pair", "dp"), None), P("dp", None)),
        check_vma=False,
    )
```

```python
import functools
import math

import jax
import jax.numpy as jnp
from jax import lax
from jax.experimental import pallas as pl
from jax.experimental.pallas import tpu as pltpu
from jax.sharding import PartitionSpec as P

inverse_temperature = 10.0
exponent_scale = 10.0 * math.log2(math.e)
epsilon = 1e-06
lanes = 128
tail = 16
f32, bf16 = jnp.float32, jnp.bfloat16


def swapped(value, axis, mask):
    count = lax.axis_size(axis)
    return lax.ppermute(value, axis, [(s, s ^ mask) for s in range(count)])


def vmem_spec():
    return pl.BlockSpec(memory_space=pltpu.VMEM)


def smem_spec():
    return pl.BlockSpec(memory_space=pltpu.SMEM)


def small_grant(mib):
    return pltpu.CompilerParams(vmem_limit_bytes=mib * 2**20)


def project_kernel(
    features_ref,
    weight_ref,
    lse_ref,
    positive_ref,
    projected_ref,
    packed_ref,
    held,
    weight,
    lse,
    positive,
    sems,
    small_sems,
):
    rows = held.shape[0]
    chunks = sems.shape[0]
    chunk = rows // chunks
    weight_copy = pltpu.make_async_copy(weight_ref, weight, small_sems.at[0])
    lse_copy = pltpu.make_async_copy(lse_ref, lse, small_sems.at[1])
    positive_copy = pltpu.make_async_copy(positive_ref, positive, small_sems.at[2])
    copies = []
    for k in range(chunks):
        part = pl.ds(k * chunk, chunk)
        copies.append(
            pltpu.make_async_copy(features_ref.at[part, :], held.at[part, :], sems.at[k])
        )
    for copy in [weight_copy] + copies + [lse_copy, positive_copy]:
        copy.start()
    weight_copy.wait()
    for k, copy in enumerate(copies):
        part = pl.ds(k * chunk, chunk)
        copy.wait()
        projected = jnp.dot(held[part, :], weight[...], preferred_element_type=f32)
        magnitude = jnp.sqrt(jnp.sum(projected * projected, axis=-1, keepdims=True) + epsilon)
        projected_ref[part, :] = projected
        packed_ref[part, :] = (projected / magnitude).astype(bf16)
    lse_copy.wait()
    positive_copy.wait()
    index = positive[...]
    packed_ref[pl.ds(rows, tail), :] = jnp.concatenate(
        [lse[...].astype(f32)]
        + [((index >> shift) & 127).astype(f32) for shift in (14, 7, 0)],
        axis=0,
    ).astype(bf16)


def project(features, weight, lse_rows, positive_rows):
    rows, units = features.shape
    width = weight.shape[1]
    chunks = 8
    hbm = pl.BlockSpec(memory_space=pltpu.HBM)
    return pl.pallas_call(
        project_kernel,
        in_specs=[hbm] * 4,
        out_specs=[vmem_spec()] * 3,
        out_shape=[
            jax.ShapeDtypeStruct((rows, width), f32),
            jax.ShapeDtypeStruct((rows + tail, width), bf16),
            jax.ShapeDtypeStruct((rows, units), bf16),
        ],
        scratch_shapes=[
            pltpu.VMEM((units, width), bf16),
            pltpu.VMEM(lse_rows.shape, lse_rows.dtype),
            pltpu.VMEM(positive_rows.shape, positive_rows.dtype),
            pltpu.SemaphoreType.DMA((chunks,)),
            pltpu.SemaphoreType.DMA((3,)),
        ],
        compiler_params=small_grant(8),
        name="project",
    )(
        *(
            pltpu.with_memory_space_constraint(value, pltpu.HBM)
            for value in (features, weight, lse_rows, positive_rows)
        )
    )


def as_columns(rows):
    return jnp.concatenate(
        [
            jnp.broadcast_to(rows[k : k + 1, :], (lanes, lanes)).T
            for k in range(rows.shape[0])
        ],
        axis=0,
    )


def coupled_rows(start, chunk, columns, base_ref, own_ref, parts, total):
    rows = own_ref.shape[0] - tail
    column = lax.broadcasted_iota(jnp.int32, (1, lanes), 1)
    own = own_ref[pl.ds(start, chunk), :]
    weight_i, positive_i = (values[start : start + chunk, :] for values in columns)
    for which, part in enumerate(parts):
        part_weight = jnp.exp(-part[pl.ds(rows, tail), :].astype(f32))
        for begin in range(0, rows, chunk):
            other = part[pl.ds(begin, chunk), :]
            cosine = lax.dot_general(
                own, other, (((1,), (1,)), ((), ())), preferred_element_type=f32
            )
            pieces = []
            for lane in range(0, chunk, lanes):
                k = (begin + lane) // lanes
                grown = jnp.exp2(cosine[:, lane : lane + lanes] * exponent_scale)
                ids = (column + (base_ref[which] + (begin + lane))).astype(f32)
                value = grown * (weight_i + part_weight[k : k + 1, :])
                value = value - jnp.where(positive_i == ids, 2.0, 0.0)
                pieces.append(value.astype(bf16))
            coupling = jnp.concatenate(pieces, axis=1)
            total = total + jnp.dot(coupling, other, preferred_element_type=f32)
    return total


def own_columns(own_ref):
    rows = own_ref.shape[0] - tail
    count = rows // lanes
    values = own_ref[pl.ds(rows, tail), :].astype(f32)
    lse, high, middle, low = (values[k * count : (k + 1) * count, :] for k in range(4))
    positive = (high * 128.0 + middle) * 128.0 + low
    return as_columns(jnp.exp(-lse)), as_columns(positive)


def couple_kernel(owners, count, base_ref, *refs):
    owns, parts, before, acc_ref = (
        refs[:owners], refs[owners : owners + count], refs[owners + count : -1], refs[-1]
    )
    rows = owns[0].shape[0] - tail
    chunk = min(256, rows)
    for k, own_ref in enumerate(owns):
        columns = own_columns(own_ref)
        for start in range(0, rows, chunk):
            part = pl.ds(start, chunk)
            total = before[0][k, part, :] if before else jnp.zeros((chunk, own_ref.shape[1]), f32)
            acc_ref[k, part, :] = coupled_rows(
                start, chunk, columns, base_ref, own_ref, parts, total
            )


def couple_cost(rows, width, count):
    pairs = rows * rows * count
    return pl.CostEstimate(
        flops=4 * pairs * width, bytes_accessed=rows * width * 4, transcendentals=pairs
    )


def couple(bases, owns, parts, before=()):
    rows, width = owns[0].shape[0] - tail, owns[0].shape[1]
    return pl.pallas_call(
        functools.partial(couple_kernel, len(owns), len(parts)),
        in_specs=[smem_spec()] + [vmem_spec()] * (len(owns) + len(parts) + len(before)),
        out_specs=vmem_spec(),
        out_shape=jax.ShapeDtypeStruct((len(owns), rows, width), f32),
        compiler_params=small_grant(8),
        cost_estimate=couple_cost(rows, width, len(parts) * len(owns)),
        name="couple",
    )(bases, *owns, *parts, *before)


def finish_kernel(count, core_ref, acc_ref, projected_ref, features_ref, *refs):
    received, grad_ref, half_ref, sends = refs[:count], refs[count], refs[count + 1], refs[count + 2 :]
    rows = projected_ref.shape[0]
    chunk = min(256, rows)
    for start in range(0, rows, chunk):
        part = pl.ds(start, chunk)
        total = acc_ref[0, part, :]
        for other in received:
            total = total + other[part, :]
        projected = projected_ref[part, :]
        magnitude = jnp.sqrt(jnp.sum(projected * projected, axis=-1, keepdims=True) + epsilon)
        unit = projected / magnitude
        upstream = total * inverse_temperature
        grad = (upstream - unit * jnp.sum(unit * upstream, axis=-1, keepdims=True)) / magnitude
        grad_ref[part, :] = grad
        half_ref[:, part] = grad.T.astype(bf16)
    for mask, send in enumerate(sends, 1):
        weight_columns(half_ref, features_ref, core_ref[0] ^ mask, send)


def weight_columns(half_ref, features_ref, share, out_ref):
    size = out_ref.shape[1]
    chunk = min(256, size)
    for start in range(0, size, chunk):
        columns = pl.ds(pl.multiple_of(share * size + start, chunk), chunk)
        out_ref[:, pl.ds(start, chunk)] = jnp.dot(
            half_ref[...], features_ref[:, columns], preferred_element_type=f32
        ).astype(out_ref.dtype)


def finish(core, acc, projected, features, received, shares):
    rows, width = projected.shape
    units = features.shape[1]
    return pl.pallas_call(
        functools.partial(finish_kernel, len(received)),
        in_specs=[smem_spec()] + [vmem_spec()] * (3 + len(received)),
        out_specs=[vmem_spec()] * (1 + shares),
        out_shape=[
            jax.ShapeDtypeStruct((rows, width), f32),
            jax.ShapeDtypeStruct((width, rows), bf16),
        ]
        + [jax.ShapeDtypeStruct((width, units // shares), bf16)] * (shares - 1),
        compiler_params=small_grant(8),
        name="finish",
    )(core[None], acc, projected, features, *received)


def weight_kernel(share_ref, half_ref, features_ref, out_ref):
    weight_columns(half_ref, features_ref, share_ref[0], out_ref)


def weight_term(half, features, share, shares):
    width, rows = half.shape
    size = features.shape[1] // shares
    return pl.pallas_call(
        weight_kernel,
        in_specs=[smem_spec()] + [vmem_spec()] * 2,
        out_specs=vmem_spec(),
        out_shape=jax.ShapeDtypeStruct((width, size), f32),
        compiler_params=small_grant(8),
        cost_estimate=pl.CostEstimate(
            flops=2 * rows * size * width, bytes_accessed=rows * size * 2, transcendentals=0
        ),
        name="weight_term",
    )(share[None], half, features)


def split_kernel(count, digit_ref, own_ref, *refs):
    parts, keep_ref, sends = refs[:count], refs[count], refs[count + 1 :]
    size = keep_ref.shape[1]
    for s in range(len(sends) + 1):
        columns = pl.ds(pl.multiple_of((digit_ref[0] ^ s) * size, size), size)
        total = own_ref[:, columns]
        for part in parts:
            total = total + part[:, columns].astype(f32)
        if s == 0:
            keep_ref[...] = total
        else:
            sends[s - 1][...] = total.astype(bf16)


def split(digit, own, parts, ways):
    width, size = own.shape[0], own.shape[1] // ways
    return pl.pallas_call(
        functools.partial(split_kernel, len(parts)),
        in_specs=[smem_spec()] + [vmem_spec()] * (1 + len(parts)),
        out_specs=[vmem_spec()] * ways,
        out_shape=[jax.ShapeDtypeStruct((width, size), f32)]
        + [jax.ShapeDtypeStruct((width, size), bf16)] * (ways - 1),
        compiler_params=small_grant(4),
        name="split",
    )(digit[None], own, *parts)


def join_kernel(digit_ref, *refs):
    parts, out_ref = refs[:-1], refs[-1]
    size = parts[0].shape[1]
    for s, part in enumerate(parts):
        rows = pl.ds(pl.multiple_of((digit_ref[0] ^ s) * size, size), size)
        out_ref[rows, :] = part[...].astype(f32).T


def join(digit, parts):
    width, size = parts[0].shape
    return pl.pallas_call(
        join_kernel,
        in_specs=[smem_spec()] + [vmem_spec()] * len(parts),
        out_specs=vmem_spec(),
        out_shape=jax.ShapeDtypeStruct((size * len(parts), width), f32),
        compiler_params=small_grant(4),
        name="join",
    )(digit[None], *parts)


def body(features, proj_weight, row_lse, positive):
    rows = features.shape[0]
    dp_count = lax.axis_size("dp")
    pair_count = lax.axis_size("pair")
    far = pair_count // 4
    group_rows = rows * dp_count
    block = lax.axis_index("pair").astype(jnp.int32)
    core = lax.axis_index("dp").astype(jnp.int32)

    lse_rows = row_lse.reshape(rows // lanes, lanes)
    positive_rows = positive.reshape(rows // lanes, lanes)
    projected, packed, held = project(features, proj_weight, lse_rows, positive_rows)

    def pairing(count, stride, odd):
        size = count // stride
        return lambda i: (((i // stride + odd) % size ^ 1) + size - odd) % size * stride + i % stride

    def partner(stride, odd):
        to = pairing(pair_count, stride, odd)
        part = lax.ppermute(packed, "pair", [(i, to(i)) for i in range(pair_count)])
        return part, to(block) * group_rows + core * rows

    (near_even, base_a), (far_even, base_b) = partner(1, 0), partner(far, 0)
    (far_odd, base_c), (near_odd, base_d) = partner(far, 1), partner(1, 1)
    siblings = [swapped(packed, "dp", mask) for mask in range(1, dp_count)]
    owns = siblings + [packed]
    acc = couple(jnp.stack([base_c]), owns, [far_odd])
    acc = couple(jnp.stack([base_a, base_b]), owns, [near_even, far_even], (acc,))
    acc_siblings = couple(jnp.stack([base_d]), siblings, [near_odd], (acc,))
    returned = [swapped(acc_siblings[mask - 1], "dp", mask) for mask in range(1, dp_count)]
    acc = couple(jnp.stack([base_d]), [packed], [near_odd], (acc[dp_count - 1 :],))
    grad_embed, half, *sends = finish(core, acc, projected, held, returned, dp_count)
    received = [swapped(send, "dp", mask) for mask, send in enumerate(sends, 1)]
    mine = weight_term(half, held, core, dp_count)

    ways = 4
    digit = block & (ways - 1)
    keep, *sends = split(digit, mine, received, ways)
    moved = [swapped(sends[s - 1], "pair", s) for s in reversed(range(1, ways))]
    for part in moved:
        keep = keep + part.astype(f32)
    stride = ways
    while stride < pair_count:
        mine = keep.astype(bf16)
        last, middle, near = (swapped(mine, "pair", s * stride).astype(f32) for s in (3, 2, 1))
        keep = (mine.astype(f32) + near) + (middle + last)
        stride *= ways
    mine = keep.astype(bf16)
    moved = [swapped(mine, "pair", s) for s in reversed(range(1, ways))]
    return (grad_embed, join(digit, [mine] + moved[::-1]))


def solution(mesh):
    return jax.shard_map(
        body,
        mesh=mesh,
        in_specs=(P(("pair", "dp"), None), P(), P(("pair", "dp")), P(("pair", "dp"))),
        out_specs=(P(("pair", "dp"), None), P("dp", None)),
        check_vma=False,
    )
```

```python
import functools
import math

import jax
import jax.numpy as jnp
from jax import lax
from jax.experimental import pallas as pl
from jax.experimental.pallas import tpu as pltpu
from jax.sharding import PartitionSpec as P

inverse_temperature = 10.0
exponent_scale = 10.0 * math.log2(math.e)
epsilon = 1e-06
lanes = 128
tail = 16
f32, bf16 = jnp.float32, jnp.bfloat16


def swapped(value, mask):
    count = lax.axis_size("dp")
    return lax.ppermute(value, "dp", [(d, d ^ mask) for d in range(count)])


def exchanged(value, mask):
    count = lax.axis_size("pair")
    return lax.ppermute(value, "pair", [(p, p ^ mask) for p in range(count)])


def crossed(value, to):
    blocks, cores = lax.axis_size("pair"), lax.axis_size("dp")
    pairs = [
        (block * cores + core, to(block) * cores + (core ^ 1))
        for block in range(blocks)
        for core in range(cores)
    ]
    return lax.ppermute(value, ("pair", "dp"), pairs)


def vmem_spec():
    return pl.BlockSpec(memory_space=pltpu.VMEM)


def smem_spec():
    return pl.BlockSpec(memory_space=pltpu.SMEM)


def small_grant(mib):
    return pltpu.CompilerParams(vmem_limit_bytes=mib * 2**20)


def project_kernel(
    features_ref,
    weight_ref,
    lse_ref,
    positive_ref,
    projected_ref,
    packed_ref,
    held,
    weight,
    lse,
    positive,
    sems,
    small_sems,
):
    rows = held.shape[0]
    chunks = sems.shape[0]
    chunk = rows // chunks
    weight_copy = pltpu.make_async_copy(weight_ref, weight, small_sems.at[0])
    lse_copy = pltpu.make_async_copy(lse_ref, lse, small_sems.at[1])
    positive_copy = pltpu.make_async_copy(positive_ref, positive, small_sems.at[2])
    copies = []
    for k in range(chunks):
        part = pl.ds(k * chunk, chunk)
        copies.append(
            pltpu.make_async_copy(features_ref.at[part, :], held.at[part, :], sems.at[k])
        )
    for copy in [weight_copy] + copies + [lse_copy, positive_copy]:
        copy.start()
    weight_copy.wait()
    for k, copy in enumerate(copies):
        part = pl.ds(k * chunk, chunk)
        copy.wait()
        projected = jnp.dot(held[part, :], weight[...], preferred_element_type=f32)
        magnitude = jnp.sqrt(jnp.sum(projected * projected, axis=-1, keepdims=True) + epsilon)
        projected_ref[part, :] = projected
        packed_ref[part, :] = (projected / magnitude).astype(bf16)
    lse_copy.wait()
    positive_copy.wait()
    index = positive[...]
    packed_ref[pl.ds(rows, tail), :] = jnp.concatenate(
        [lse[...].astype(f32)]
        + [((index >> shift) & 127).astype(f32) for shift in (14, 7, 0)],
        axis=0,
    ).astype(bf16)


def project(features, weight, lse_rows, positive_rows):
    rows, units = features.shape
    width = weight.shape[1]
    chunks = 2
    hbm = pl.BlockSpec(memory_space=pltpu.HBM)
    return pl.pallas_call(
        project_kernel,
        in_specs=[hbm] * 4,
        out_specs=[vmem_spec()] * 3,
        out_shape=[
            jax.ShapeDtypeStruct((rows, width), f32),
            jax.ShapeDtypeStruct((rows + tail, width), bf16),
            jax.ShapeDtypeStruct((rows, units), bf16),
        ],
        scratch_shapes=[
            pltpu.VMEM((units, width), bf16),
            pltpu.VMEM(lse_rows.shape, lse_rows.dtype),
            pltpu.VMEM(positive_rows.shape, positive_rows.dtype),
            pltpu.SemaphoreType.DMA((chunks,)),
            pltpu.SemaphoreType.DMA((3,)),
        ],
        compiler_params=small_grant(8),
        name="project",
    )(
        *(
            pltpu.with_memory_space_constraint(value, pltpu.HBM)
            for value in (features, weight, lse_rows, positive_rows)
        )
    )


def as_columns(rows):
    return jnp.concatenate(
        [
            jnp.broadcast_to(rows[k : k + 1, :], (lanes, lanes)).T
            for k in range(rows.shape[0])
        ],
        axis=0,
    )


def coupled_rows(start, chunk, columns, base_ref, own_ref, parts, total):
    rows = own_ref.shape[0] - tail
    column = lax.broadcasted_iota(jnp.int32, (1, lanes), 1)
    own = own_ref[pl.ds(start, chunk), :]
    weight_i, positive_i = (values[start : start + chunk, :] for values in columns)
    for which, part in enumerate(parts):
        part_weight = jnp.exp(-part[pl.ds(rows, tail), :].astype(f32))
        for begin in range(0, rows, chunk):
            other = part[pl.ds(begin, chunk), :]
            cosine = lax.dot_general(
                own, other, (((1,), (1,)), ((), ())), preferred_element_type=f32
            )
            pieces = []
            for lane in range(0, chunk, lanes):
                k = (begin + lane) // lanes
                grown = jnp.exp2(cosine[:, lane : lane + lanes] * exponent_scale)
                ids = (column + (base_ref[which] + (begin + lane))).astype(f32)
                value = grown * (weight_i + part_weight[k : k + 1, :])
                value = value - jnp.where(positive_i == ids, 2.0, 0.0)
                pieces.append(value.astype(bf16))
            coupling = jnp.concatenate(pieces, axis=1)
            total = total + jnp.dot(coupling, other, preferred_element_type=f32)
    return total


def own_columns(own_ref):
    rows = own_ref.shape[0] - tail
    count = rows // lanes
    values = own_ref[pl.ds(rows, tail), :].astype(f32)
    lse, high, middle, low = (values[k * count : (k + 1) * count, :] for k in range(4))
    positive = (high * 128.0 + middle) * 128.0 + low
    return as_columns(jnp.exp(-lse)), as_columns(positive)


def couple_kernel(owners, count, base_ref, *refs):
    owns, parts, before, acc_ref = (
        refs[:owners], refs[owners : owners + count], refs[owners + count : -1], refs[-1]
    )
    rows = owns[0].shape[0] - tail
    chunk = min(256, rows)
    for k, own_ref in enumerate(owns):
        columns = own_columns(own_ref)
        for start in range(0, rows, chunk):
            part = pl.ds(start, chunk)
            total = before[0][k, part, :] if before else jnp.zeros((chunk, own_ref.shape[1]), f32)
            acc_ref[k, part, :] = coupled_rows(
                start, chunk, columns, base_ref, own_ref, parts, total
            )


def couple_cost(rows, width, count):
    pairs = rows * rows * count
    return pl.CostEstimate(
        flops=4 * pairs * width, bytes_accessed=rows * width * 4, transcendentals=pairs
    )


def couple(bases, owns, parts, before=()):
    rows, width = owns[0].shape[0] - tail, owns[0].shape[1]
    return pl.pallas_call(
        functools.partial(couple_kernel, len(owns), len(parts)),
        in_specs=[smem_spec()] + [vmem_spec()] * (len(owns) + len(parts) + len(before)),
        out_specs=vmem_spec(),
        out_shape=jax.ShapeDtypeStruct((len(owns), rows, width), f32),
        compiler_params=small_grant(8),
        cost_estimate=couple_cost(rows, width, len(parts) * len(owns)),
        name="couple",
    )(bases, *owns, *parts, *before)


def finish_kernel(count, core_ref, acc_ref, projected_ref, features_ref, *refs):
    received, grad_ref, half_ref, sends = refs[:count], refs[count], refs[count + 1], refs[count + 2 :]
    rows = projected_ref.shape[0]
    chunk = min(256, rows)
    for start in range(0, rows, chunk):
        part = pl.ds(start, chunk)
        total = acc_ref[0, part, :]
        for other in received:
            total = total + other[part, :]
        projected = projected_ref[part, :]
        magnitude = jnp.sqrt(jnp.sum(projected * projected, axis=-1, keepdims=True) + epsilon)
        unit = projected / magnitude
        upstream = total * inverse_temperature
        grad = (upstream - unit * jnp.sum(unit * upstream, axis=-1, keepdims=True)) / magnitude
        grad_ref[part, :] = grad
        half_ref[:, part] = grad.T.astype(bf16)
    for mask, send in enumerate(sends, 1):
        weight_columns(half_ref, features_ref, core_ref[0] ^ mask, send)


def weight_columns(half_ref, features_ref, share, out_ref):
    size = out_ref.shape[1]
    chunk = min(256, size)
    for start in range(0, size, chunk):
        columns = pl.ds(pl.multiple_of(share * size + start, chunk), chunk)
        out_ref[:, pl.ds(start, chunk)] = jnp.dot(
            half_ref[...], features_ref[:, columns], preferred_element_type=f32
        ).astype(out_ref.dtype)


def finish(core, acc, projected, features, received, shares):
    rows, width = projected.shape
    units = features.shape[1]
    return pl.pallas_call(
        functools.partial(finish_kernel, len(received)),
        in_specs=[smem_spec()] + [vmem_spec()] * (3 + len(received)),
        out_specs=[vmem_spec()] * (1 + shares),
        out_shape=[
            jax.ShapeDtypeStruct((rows, width), f32),
            jax.ShapeDtypeStruct((width, rows), bf16),
        ]
        + [jax.ShapeDtypeStruct((width, units // shares), bf16)] * (shares - 1),
        compiler_params=small_grant(8),
        name="finish",
    )(core[None], acc, projected, features, *received)


def weight_kernel(share_ref, half_ref, features_ref, out_ref):
    weight_columns(half_ref, features_ref, share_ref[0], out_ref)


def weight_term(half, features, share, shares):
    width, rows = half.shape
    size = features.shape[1] // shares
    return pl.pallas_call(
        weight_kernel,
        in_specs=[smem_spec()] + [vmem_spec()] * 2,
        out_specs=vmem_spec(),
        out_shape=jax.ShapeDtypeStruct((width, size), f32),
        compiler_params=small_grant(8),
        cost_estimate=pl.CostEstimate(
            flops=2 * rows * size * width, bytes_accessed=rows * size * 2, transcendentals=0
        ),
        name="weight_term",
    )(share[None], half, features)


def split_kernel(count, digit_ref, own_ref, *refs):
    parts, keep_ref, sends = refs[:count], refs[count], refs[count + 1 :]
    size = keep_ref.shape[1]
    for s in range(len(sends) + 1):
        columns = pl.ds(pl.multiple_of((digit_ref[0] ^ s) * size, size), size)
        total = own_ref[:, columns]
        for part in parts:
            total = total + part[:, columns].astype(f32)
        if s == 0:
            keep_ref[...] = total
        else:
            sends[s - 1][...] = total.astype(bf16)


def split(digit, own, parts, ways):
    width, size = own.shape[0], own.shape[1] // ways
    return pl.pallas_call(
        functools.partial(split_kernel, len(parts)),
        in_specs=[smem_spec()] + [vmem_spec()] * (1 + len(parts)),
        out_specs=[vmem_spec()] * ways,
        out_shape=[jax.ShapeDtypeStruct((width, size), f32)]
        + [jax.ShapeDtypeStruct((width, size), bf16)] * (ways - 1),
        compiler_params=small_grant(4),
        name="split",
    )(digit[None], own, *parts)


def join_kernel(digit_ref, *refs):
    parts, out_ref = refs[:-1], refs[-1]
    size = parts[0].shape[1]
    for s, part in enumerate(reversed(parts)):
        rows = pl.ds(pl.multiple_of((digit_ref[0] ^ s) * size, size), size)
        out_ref[rows, :] = part[...].astype(f32).T


def join(digit, parts):
    width, size = parts[0].shape
    return pl.pallas_call(
        join_kernel,
        in_specs=[smem_spec()] + [vmem_spec()] * len(parts),
        out_specs=vmem_spec(),
        out_shape=jax.ShapeDtypeStruct((size * len(parts), width), f32),
        compiler_params=small_grant(4),
        name="join",
    )(digit[None], *parts)


def body(features, proj_weight, row_lse, positive):
    rows = features.shape[0]
    dp_count = lax.axis_size("dp")
    pair_count = lax.axis_size("pair")
    far = pair_count // 4
    group_rows = rows * dp_count
    block = lax.axis_index("pair").astype(jnp.int32)
    core = lax.axis_index("dp").astype(jnp.int32)

    lse_rows = row_lse.reshape(rows // lanes, lanes)
    positive_rows = positive.reshape(rows // lanes, lanes)
    projected, packed, held = project(features, proj_weight, lse_rows, positive_rows)

    def pairing(count, stride, odd):
        size = count // stride
        return lambda i: (((i // stride + odd) % size ^ 1) + size - odd) % size * stride + i % stride

    def partner(stride, odd):
        to = pairing(pair_count, stride, odd)
        return crossed(packed, to), to(block) * group_rows + (core ^ 1) * rows

    (near_even, base_a), (far_even, base_b) = partner(1, 0), partner(far, 0)
    (far_odd, base_c), (near_odd, base_d) = partner(far, 1), partner(1, 1)
    siblings = [swapped(packed, mask) for mask in range(1, dp_count)]
    owns = siblings + [packed]
    acc = couple(jnp.stack([base_c]), owns, [far_odd])
    acc = couple(jnp.stack([base_a, base_b]), owns, [near_even, far_even], (acc,))
    acc_siblings = couple(jnp.stack([base_d]), siblings, [near_odd], (acc,))
    returned = [swapped(acc_siblings[mask - 1], mask) for mask in range(1, dp_count)]
    acc = couple(jnp.stack([base_d]), [packed], [near_odd], (acc[dp_count - 1 :],))
    grad_embed, half, *sends = finish(core, acc, projected, held, returned, dp_count)
    received = [swapped(send, mask) for mask, send in enumerate(sends, 1)]
    mine = weight_term(half, held, core, dp_count)

    ways = 4
    digit = block & (ways - 1)
    keep, *sends = split(digit, mine, received, ways)
    moved = [exchanged(sends[s - 1], s) for s in reversed(range(1, ways))]
    for part in moved:
        keep = keep + part.astype(f32)
    stride = ways
    while stride < pair_count:
        mine = keep.astype(bf16)
        last, middle, near = (exchanged(mine, s * stride).astype(f32) for s in (3, 2, 1))
        keep = (last + middle) + (near + mine.astype(f32))
        stride *= ways
    mine = keep.astype(bf16)
    moved = [exchanged(mine, s) for s in reversed(range(1, ways))]
    return (grad_embed, join(digit, moved + [mine]))


def solution(mesh):
    return jax.shard_map(
        body,
        mesh=mesh,
        in_specs=(P(("pair", "dp"), None), P(), P(("pair", "dp")), P(("pair", "dp"))),
        out_specs=(P(("pair", "dp"), None), P("dp", None)),
        check_vma=False,
    )
```

```python
import functools
import math

import jax
import jax.numpy as jnp
from jax import lax
from jax.experimental import pallas as pl
from jax.experimental.pallas import tpu as pltpu
from jax.sharding import PartitionSpec as P

inverse_temperature = 10.0
exponent_scale = 10.0 * math.log2(math.e)
epsilon = 1e-06
lanes = 128
tail = 16
f32, bf16 = jnp.float32, jnp.bfloat16


def swapped(value, mask):
    count = lax.axis_size("dp")
    return lax.ppermute(value, "dp", [(d, d ^ mask) for d in range(count)])


def exchanged(value, mask):
    count = lax.axis_size("pair")
    return lax.ppermute(value, "pair", [(p, p ^ mask) for p in range(count)])


def crossed(value, to):
    blocks, cores = lax.axis_size("pair"), lax.axis_size("dp")
    pairs = [
        (block * cores + core, to(block) * cores + (core ^ 1))
        for block in range(blocks)
        for core in range(cores)
    ]
    return lax.ppermute(value, ("pair", "dp"), pairs)


def vmem_spec():
    return pl.BlockSpec(memory_space=pltpu.VMEM)


def smem_spec():
    return pl.BlockSpec(memory_space=pltpu.SMEM)


def small_grant(mib):
    return pltpu.CompilerParams(vmem_limit_bytes=mib * 2**20)


def project_kernel(
    features_ref,
    weight_ref,
    lse_ref,
    positive_ref,
    projected_ref,
    packed_ref,
    held,
    weight,
    lse,
    positive,
    sems,
    small_sems,
):
    rows = held.shape[0]
    chunks = sems.shape[0]
    chunk = rows // chunks
    weight_copy = pltpu.make_async_copy(weight_ref, weight, small_sems.at[0])
    lse_copy = pltpu.make_async_copy(lse_ref, lse, small_sems.at[1])
    positive_copy = pltpu.make_async_copy(positive_ref, positive, small_sems.at[2])
    copies = []
    for k in range(chunks):
        part = pl.ds(k * chunk, chunk)
        copies.append(
            pltpu.make_async_copy(features_ref.at[part, :], held.at[part, :], sems.at[k])
        )
    for copy in [weight_copy] + copies + [lse_copy, positive_copy]:
        copy.start()
    weight_copy.wait()
    for k, copy in enumerate(copies):
        part = pl.ds(k * chunk, chunk)
        copy.wait()
        projected = jnp.dot(held[part, :], weight[...], preferred_element_type=f32)
        magnitude = jnp.sqrt(jnp.sum(projected * projected, axis=-1, keepdims=True) + epsilon)
        projected_ref[part, :] = projected
        packed_ref[part, :] = (projected / magnitude).astype(bf16)
    lse_copy.wait()
    positive_copy.wait()
    index = positive[...]
    packed_ref[pl.ds(rows, tail), :] = jnp.concatenate(
        [lse[...].astype(f32)]
        + [((index >> shift) & 127).astype(f32) for shift in (14, 7, 0)],
        axis=0,
    ).astype(bf16)


def project(features, weight, lse_rows, positive_rows):
    rows, units = features.shape
    width = weight.shape[1]
    chunks = 2
    hbm = pl.BlockSpec(memory_space=pltpu.HBM)
    return pl.pallas_call(
        project_kernel,
        in_specs=[hbm] * 4,
        out_specs=[vmem_spec()] * 3,
        out_shape=[
            jax.ShapeDtypeStruct((rows, width), f32),
            jax.ShapeDtypeStruct((rows + tail, width), bf16),
            jax.ShapeDtypeStruct((rows, units), bf16),
        ],
        scratch_shapes=[
            pltpu.VMEM((units, width), bf16),
            pltpu.VMEM(lse_rows.shape, lse_rows.dtype),
            pltpu.VMEM(positive_rows.shape, positive_rows.dtype),
            pltpu.SemaphoreType.DMA((chunks,)),
            pltpu.SemaphoreType.DMA((3,)),
        ],
        compiler_params=small_grant(8),
        name="project",
    )(
        *(
            pltpu.with_memory_space_constraint(value, pltpu.HBM)
            for value in (features, weight, lse_rows, positive_rows)
        )
    )


def as_columns(rows):
    return jnp.concatenate(
        [
            jnp.broadcast_to(rows[k : k + 1, :], (lanes, lanes)).T
            for k in range(rows.shape[0])
        ],
        axis=0,
    )


def coupled_rows(columns, base_ref, own_ref, parts, total):
    rows = own_ref.shape[0] - tail
    step = min(256, rows)
    column = lax.broadcasted_iota(jnp.int32, (1, lanes), 1)
    own = own_ref[pl.ds(0, rows), :]
    weight_i, positive_i = columns
    for which, part in enumerate(parts):
        part_weight = jnp.exp(-part[pl.ds(rows, tail), :].astype(f32))
        for begin in range(0, rows, step):
            other = part[pl.ds(begin, step), :]
            cosine = lax.dot_general(
                own, other, (((1,), (1,)), ((), ())), preferred_element_type=f32
            )
            pieces = []
            for lane in range(0, step, lanes):
                k = (begin + lane) // lanes
                grown = jnp.exp2(cosine[:, lane : lane + lanes] * exponent_scale)
                ids = (column + (base_ref[which] + (begin + lane))).astype(f32)
                value = grown * (weight_i + part_weight[k : k + 1, :])
                value = value - jnp.where(positive_i == ids, 2.0, 0.0)
                pieces.append(value.astype(bf16))
            coupling = jnp.concatenate(pieces, axis=1)
            total = total + jnp.dot(coupling, other, preferred_element_type=f32)
    return total


def own_columns(own_ref):
    rows = own_ref.shape[0] - tail
    count = rows // lanes
    values = own_ref[pl.ds(rows, tail), :].astype(f32)
    lse, high, middle, low = (values[k * count : (k + 1) * count, :] for k in range(4))
    positive = (high * 128.0 + middle) * 128.0 + low
    return as_columns(jnp.exp(-lse)), as_columns(positive)


def couple_kernel(owners, count, base_ref, *refs):
    owns, parts, before, acc_ref = (
        refs[:owners], refs[owners : owners + count], refs[owners + count : -1], refs[-1]
    )
    rows = owns[0].shape[0] - tail
    for k, own_ref in enumerate(owns):
        columns = own_columns(own_ref)
        total = before[0][k] if before else jnp.zeros((rows, own_ref.shape[1]), f32)
        acc_ref[k] = coupled_rows(columns, base_ref, own_ref, parts, total)


def couple_cost(rows, width, count):
    pairs = rows * rows * count
    return pl.CostEstimate(
        flops=4 * pairs * width, bytes_accessed=rows * width * 4, transcendentals=pairs
    )


def couple(bases, owns, parts, before=()):
    rows, width = owns[0].shape[0] - tail, owns[0].shape[1]
    return pl.pallas_call(
        functools.partial(couple_kernel, len(owns), len(parts)),
        in_specs=[smem_spec()] + [vmem_spec()] * (len(owns) + len(parts) + len(before)),
        out_specs=vmem_spec(),
        out_shape=jax.ShapeDtypeStruct((len(owns), rows, width), f32),
        compiler_params=small_grant(8),
        cost_estimate=couple_cost(rows, width, len(parts) * len(owns)),
        name="couple",
    )(bases, *owns, *parts, *before)


def finish_kernel(count, core_ref, acc_ref, projected_ref, features_ref, *refs):
    received, grad_ref, half_ref, sends = refs[:count], refs[count], refs[count + 1], refs[count + 2 :]
    rows = projected_ref.shape[0]
    chunk = min(256, rows)
    for start in range(0, rows, chunk):
        part = pl.ds(start, chunk)
        total = acc_ref[0, part, :]
        for other in received:
            total = total + other[part, :]
        projected = projected_ref[part, :]
        magnitude = jnp.sqrt(jnp.sum(projected * projected, axis=-1, keepdims=True) + epsilon)
        unit = projected / magnitude
        upstream = total * inverse_temperature
        grad = (upstream - unit * jnp.sum(unit * upstream, axis=-1, keepdims=True)) / magnitude
        grad_ref[part, :] = grad
        half_ref[:, part] = grad.T.astype(bf16)
    for mask, send in enumerate(sends, 1):
        weight_columns(half_ref, features_ref, core_ref[0] ^ mask, send)


def weight_columns(half_ref, features_ref, share, out_ref):
    size = out_ref.shape[1]
    chunk = min(256, size)
    for start in range(0, size, chunk):
        columns = pl.ds(pl.multiple_of(share * size + start, chunk), chunk)
        out_ref[:, pl.ds(start, chunk)] = jnp.dot(
            half_ref[...], features_ref[:, columns], preferred_element_type=f32
        ).astype(out_ref.dtype)


def finish(core, acc, projected, features, received, shares):
    rows, width = projected.shape
    units = features.shape[1]
    return pl.pallas_call(
        functools.partial(finish_kernel, len(received)),
        in_specs=[smem_spec()] + [vmem_spec()] * (3 + len(received)),
        out_specs=[vmem_spec()] * (1 + shares),
        out_shape=[
            pltpu.VMEM((rows, width), f32),
            jax.ShapeDtypeStruct((width, rows), bf16),
        ]
        + [jax.ShapeDtypeStruct((width, units // shares), bf16)] * (shares - 1),
        compiler_params=small_grant(8),
        name="finish",
    )(core[None], acc, projected, features, *received)


def weight_kernel(share_ref, half_ref, features_ref, out_ref):
    weight_columns(half_ref, features_ref, share_ref[0], out_ref)


def weight_term(half, features, share, shares):
    width, rows = half.shape
    size = features.shape[1] // shares
    return pl.pallas_call(
        weight_kernel,
        in_specs=[smem_spec()] + [vmem_spec()] * 2,
        out_specs=vmem_spec(),
        out_shape=jax.ShapeDtypeStruct((width, size), f32),
        compiler_params=small_grant(8),
        cost_estimate=pl.CostEstimate(
            flops=2 * rows * size * width, bytes_accessed=rows * size * 2, transcendentals=0
        ),
        name="weight_term",
    )(share[None], half, features)


def split_kernel(count, digit_ref, own_ref, *refs):
    parts, keep_ref, sends = refs[:count], refs[count], refs[count + 1 :]
    size = keep_ref.shape[1]
    for s in range(len(sends) + 1):
        columns = pl.ds(pl.multiple_of((digit_ref[0] ^ s) * size, size), size)
        total = own_ref[:, columns]
        for part in parts:
            total = total + part[:, columns].astype(f32)
        if s == 0:
            keep_ref[...] = total
        else:
            sends[s - 1][...] = total.astype(bf16)


def split(digit, own, parts, ways):
    width, size = own.shape[0], own.shape[1] // ways
    return pl.pallas_call(
        functools.partial(split_kernel, len(parts)),
        in_specs=[smem_spec()] + [vmem_spec()] * (1 + len(parts)),
        out_specs=[vmem_spec()] * ways,
        out_shape=[jax.ShapeDtypeStruct((width, size), f32)]
        + [jax.ShapeDtypeStruct((width, size), bf16)] * (ways - 1),
        compiler_params=small_grant(4),
        name="split",
    )(digit[None], own, *parts)


def join_kernel(digit_ref, *refs):
    parts, out_ref = refs[:-1], refs[-1]
    size = parts[0].shape[1]
    for s, part in enumerate(reversed(parts)):
        rows = pl.ds(pl.multiple_of((digit_ref[0] ^ s) * size, size), size)
        out_ref[rows, :] = part[...].astype(f32).T


def join(digit, parts):
    width, size = parts[0].shape
    return pl.pallas_call(
        join_kernel,
        in_specs=[smem_spec()] + [vmem_spec()] * len(parts),
        out_specs=vmem_spec(),
        out_shape=jax.ShapeDtypeStruct((size * len(parts), width), f32),
        compiler_params=small_grant(4),
        name="join",
    )(digit[None], *parts)


def body(features, proj_weight, row_lse, positive):
    rows = features.shape[0]
    dp_count = lax.axis_size("dp")
    pair_count = lax.axis_size("pair")
    far = pair_count // 4
    group_rows = rows * dp_count
    block = lax.axis_index("pair").astype(jnp.int32)
    core = lax.axis_index("dp").astype(jnp.int32)

    lse_rows = row_lse.reshape(rows // lanes, lanes)
    positive_rows = positive.reshape(rows // lanes, lanes)
    projected, packed, held = project(features, proj_weight, lse_rows, positive_rows)

    def pairing(count, stride, odd):
        size = count // stride
        return lambda i: (((i // stride + odd) % size ^ 1) + size - odd) % size * stride + i % stride

    def partner(stride, odd):
        to = pairing(pair_count, stride, odd)
        return crossed(packed, to), to(block) * group_rows + (core ^ 1) * rows

    (near_even, base_a), (far_even, base_b) = partner(1, 0), partner(far, 0)
    (far_odd, base_c), (near_odd, base_d) = partner(far, 1), partner(1, 1)
    siblings = [swapped(packed, mask) for mask in range(1, dp_count)]
    owns = siblings + [packed]
    acc = couple(jnp.stack([base_c]), owns, [far_odd])
    acc = couple(jnp.stack([base_a, base_b]), owns, [near_even, far_even], (acc,))
    acc_siblings = couple(jnp.stack([base_d]), siblings, [near_odd], (acc,))
    returned = [swapped(acc_siblings[mask - 1], mask) for mask in range(1, dp_count)]
    acc = couple(jnp.stack([base_d]), [packed], [near_odd], (acc[dp_count - 1 :],))
    grad_embed, half, *sends = finish(core, acc, projected, held, returned, dp_count)
    received = [swapped(send, mask) for mask, send in enumerate(sends, 1)]
    mine = weight_term(half, held, core, dp_count)

    ways = 4
    digit = block & (ways - 1)
    keep, *sends = split(digit, mine, received, ways)
    moved = [exchanged(sends[s - 1], s) for s in reversed(range(1, ways))]
    for part in moved:
        keep = keep + part.astype(f32)
    stride = ways
    while stride < pair_count:
        mine = keep.astype(bf16)
        last, middle, near = (exchanged(mine, s * stride).astype(f32) for s in (3, 2, 1))
        keep = (last + middle) + (near + mine.astype(f32))
        stride *= ways
    mine = keep.astype(bf16)
    moved = [exchanged(mine, s) for s in reversed(range(1, ways))]
    return (grad_embed, join(digit, moved + [mine]))


def solution(mesh):
    return jax.shard_map(
        body,
        mesh=mesh,
        in_specs=(P(("pair", "dp"), None), P(), P(("pair", "dp")), P(("pair", "dp"))),
        out_specs=(P(("pair", "dp"), None), P("dp", None)),
        check_vma=False,
    )
```

```python
import functools
import math

import jax
import jax.numpy as jnp
from jax import lax
from jax.experimental import pallas as pl
from jax.experimental.pallas import tpu as pltpu
from jax.sharding import PartitionSpec as P

inverse_temperature = 10.0
exponent_scale = 10.0 * math.log2(math.e)
epsilon = 1e-06
lanes = 128
tail = 16
f32, bf16 = jnp.float32, jnp.bfloat16


def swapped(value, mask):
    count = lax.axis_size("dp")
    return lax.ppermute(value, "dp", [(d, d ^ mask) for d in range(count)])


def exchanged(value, mask):
    count = lax.axis_size("pair")
    return lax.ppermute(value, "pair", [(p, p ^ mask) for p in range(count)])


def crossed(value, to, turn=1):
    blocks, cores = lax.axis_size("pair"), lax.axis_size("dp")
    pairs = [
        (block * cores + core, to(block) * cores + (core ^ turn))
        for block in range(blocks)
        for core in range(cores)
    ]
    return lax.ppermute(value, ("pair", "dp"), pairs)


def vmem_spec():
    return pl.BlockSpec(memory_space=pltpu.VMEM)


def smem_spec():
    return pl.BlockSpec(memory_space=pltpu.SMEM)


def small_grant(mib):
    return pltpu.CompilerParams(vmem_limit_bytes=mib * 2**20)


def project_kernel(
    features_ref,
    weight_ref,
    lse_ref,
    positive_ref,
    projected_ref,
    packed_ref,
    held,
    weight,
    lse,
    positive,
    sems,
    small_sems,
):
    rows = held.shape[0]
    chunks = sems.shape[0]
    chunk = rows // chunks
    weight_copy = pltpu.make_async_copy(weight_ref, weight, small_sems.at[0])
    lse_copy = pltpu.make_async_copy(lse_ref, lse, small_sems.at[1])
    positive_copy = pltpu.make_async_copy(positive_ref, positive, small_sems.at[2])
    copies = []
    for k in range(chunks):
        part = pl.ds(k * chunk, chunk)
        copies.append(
            pltpu.make_async_copy(features_ref.at[part, :], held.at[part, :], sems.at[k])
        )
    for copy in [weight_copy] + copies + [lse_copy, positive_copy]:
        copy.start()
    weight_copy.wait()
    for k, copy in enumerate(copies):
        part = pl.ds(k * chunk, chunk)
        copy.wait()
        projected = jnp.dot(held[part, :], weight[...], preferred_element_type=f32)
        magnitude = jnp.sqrt(jnp.sum(projected * projected, axis=-1, keepdims=True) + epsilon)
        projected_ref[part, :] = projected
        packed_ref[part, :] = (projected / magnitude).astype(bf16)
    lse_copy.wait()
    positive_copy.wait()
    index = positive[...]
    packed_ref[pl.ds(rows, tail), :] = jnp.concatenate(
        [lse[...].astype(f32)]
        + [((index >> shift) & 127).astype(f32) for shift in (14, 7, 0)],
        axis=0,
    ).astype(bf16)


def project(features, weight, lse_rows, positive_rows):
    rows, units = features.shape
    width = weight.shape[1]
    chunks = 2
    hbm = pl.BlockSpec(memory_space=pltpu.HBM)
    return pl.pallas_call(
        project_kernel,
        in_specs=[hbm] * 4,
        out_specs=[vmem_spec()] * 3,
        out_shape=[
            jax.ShapeDtypeStruct((rows, width), f32),
            jax.ShapeDtypeStruct((rows + tail, width), bf16),
            jax.ShapeDtypeStruct((rows, units), bf16),
        ],
        scratch_shapes=[
            pltpu.VMEM((units, width), bf16),
            pltpu.VMEM(lse_rows.shape, lse_rows.dtype),
            pltpu.VMEM(positive_rows.shape, positive_rows.dtype),
            pltpu.SemaphoreType.DMA((chunks,)),
            pltpu.SemaphoreType.DMA((3,)),
        ],
        compiler_params=small_grant(8),
        name="project",
    )(
        *(
            pltpu.with_memory_space_constraint(value, pltpu.HBM)
            for value in (features, weight, lse_rows, positive_rows)
        )
    )


def as_columns(rows):
    return jnp.concatenate(
        [
            jnp.broadcast_to(rows[k : k + 1, :], (lanes, lanes)).T
            for k in range(rows.shape[0])
        ],
        axis=0,
    )


def coupled_rows(columns, bases, own_ref, parts, total):
    rows = own_ref.shape[0] - tail
    step = min(256, rows)
    column = lax.broadcasted_iota(jnp.int32, (1, lanes), 1)
    own = own_ref[pl.ds(0, rows), :]
    weight_i, positive_i = columns
    for which, part in enumerate(parts):
        part_weight = jnp.exp(-part[pl.ds(rows, tail), :].astype(f32))
        for begin in range(0, rows, step):
            other = part[pl.ds(begin, step), :]
            cosine = lax.dot_general(
                own, other, (((1,), (1,)), ((), ())), preferred_element_type=f32
            )
            pieces = []
            for lane in range(0, step, lanes):
                k = (begin + lane) // lanes
                grown = jnp.exp2(cosine[:, lane : lane + lanes] * exponent_scale)
                ids = (column + (bases[which][0] + (begin + lane))).astype(f32)
                value = grown * (weight_i + part_weight[k : k + 1, :])
                value = value - jnp.where(positive_i == ids, 2.0, 0.0)
                pieces.append(value.astype(bf16))
            coupling = jnp.concatenate(pieces, axis=1)
            total = total + jnp.dot(coupling, other, preferred_element_type=f32)
    return total


def own_columns(own_ref):
    rows = own_ref.shape[0] - tail
    count = rows // lanes
    values = own_ref[pl.ds(rows, tail), :].astype(f32)
    lse, high, middle, low = (values[k * count : (k + 1) * count, :] for k in range(4))
    positive = (high * 128.0 + middle) * 128.0 + low
    return as_columns(jnp.exp(-lse)), as_columns(positive)


def couple_kernel(owners, count, *refs):
    bases, refs = refs[:count], refs[count:]
    owns, parts, before, acc_ref = (
        refs[:owners], refs[owners : owners + count], refs[owners + count : -1], refs[-1]
    )
    rows = owns[0].shape[0] - tail
    for k, own_ref in enumerate(owns):
        columns = own_columns(own_ref)
        total = before[0][k] if before else jnp.zeros((rows, own_ref.shape[1]), f32)
        acc_ref[k] = coupled_rows(columns, bases, own_ref, parts, total)


def couple_cost(rows, width, count):
    pairs = rows * rows * count
    return pl.CostEstimate(
        flops=4 * pairs * width, bytes_accessed=rows * width * 4, transcendentals=pairs
    )


def couple(bases, owns, parts, before=()):
    rows, width = owns[0].shape[0] - tail, owns[0].shape[1]
    return pl.pallas_call(
        functools.partial(couple_kernel, len(owns), len(parts)),
        in_specs=[smem_spec()] * len(parts) + [vmem_spec()] * (len(owns) + len(parts) + len(before)),
        out_specs=vmem_spec(),
        out_shape=jax.ShapeDtypeStruct((len(owns), rows, width), f32),
        compiler_params=small_grant(8),
        cost_estimate=couple_cost(rows, width, len(parts) * len(owns)),
        name="couple",
    )(*(base[None] for base in bases), *owns, *parts, *before)


def finish_kernel(count, core_ref, acc_ref, projected_ref, features_ref, *refs):
    received, grad_ref, half_ref, sends = refs[:count], refs[count], refs[count + 1], refs[count + 2 :]
    rows = projected_ref.shape[0]
    chunk = min(256, rows)
    for start in range(0, rows, chunk):
        part = pl.ds(start, chunk)
        total = acc_ref[0, part, :]
        for other in received:
            total = total + other[part, :]
        projected = projected_ref[part, :]
        magnitude = jnp.sqrt(jnp.sum(projected * projected, axis=-1, keepdims=True) + epsilon)
        unit = projected / magnitude
        upstream = total * inverse_temperature
        grad = (upstream - unit * jnp.sum(unit * upstream, axis=-1, keepdims=True)) / magnitude
        grad_ref[part, :] = grad
        half_ref[:, part] = grad.T.astype(bf16)
    for mask, send in enumerate(sends, 1):
        weight_columns(half_ref, features_ref, core_ref[0] ^ mask, send)


def weight_columns(half_ref, features_ref, share, out_ref):
    size = out_ref.shape[1]
    chunk = min(256, size)
    for start in range(0, size, chunk):
        columns = pl.ds(pl.multiple_of(share * size + start, chunk), chunk)
        out_ref[:, pl.ds(start, chunk)] = jnp.dot(
            half_ref[...], features_ref[:, columns], preferred_element_type=f32
        ).astype(out_ref.dtype)


def finish(core, acc, projected, features, received, shares):
    rows, width = projected.shape
    units = features.shape[1]
    return pl.pallas_call(
        functools.partial(finish_kernel, len(received)),
        in_specs=[smem_spec()] + [vmem_spec()] * (3 + len(received)),
        out_specs=[vmem_spec()] * (1 + shares),
        out_shape=[
            pltpu.VMEM((rows, width), f32),
            jax.ShapeDtypeStruct((width, rows), bf16),
        ]
        + [jax.ShapeDtypeStruct((width, units // shares), bf16)] * (shares - 1),
        compiler_params=small_grant(8),
        name="finish",
    )(core[None], acc, projected, features, *received)


def weight_kernel(share_ref, half_ref, features_ref, out_ref):
    weight_columns(half_ref, features_ref, share_ref[0], out_ref)


def weight_term(half, features, share, shares):
    width, rows = half.shape
    size = features.shape[1] // shares
    return pl.pallas_call(
        weight_kernel,
        in_specs=[smem_spec()] + [vmem_spec()] * 2,
        out_specs=vmem_spec(),
        out_shape=jax.ShapeDtypeStruct((width, size), f32),
        compiler_params=small_grant(8),
        cost_estimate=pl.CostEstimate(
            flops=2 * rows * size * width, bytes_accessed=rows * size * 2, transcendentals=0
        ),
        name="weight_term",
    )(share[None], half, features)


def split_kernel(count, digit_ref, own_ref, *refs):
    parts, keep_ref, sends = refs[:count], refs[count], refs[count + 1 :]
    size = keep_ref.shape[1]
    for s in range(len(sends) + 1):
        columns = pl.ds(pl.multiple_of((digit_ref[0] ^ s) * size, size), size)
        total = own_ref[:, columns]
        for part in parts:
            total = total + part[:, columns].astype(f32)
        if s == 0:
            keep_ref[...] = total
        else:
            sends[s - 1][...] = total.astype(bf16)


def split(digit, own, parts, ways):
    width, size = own.shape[0], own.shape[1] // ways
    return pl.pallas_call(
        functools.partial(split_kernel, len(parts)),
        in_specs=[smem_spec()] + [vmem_spec()] * (1 + len(parts)),
        out_specs=[vmem_spec()] * ways,
        out_shape=[jax.ShapeDtypeStruct((width, size), f32)]
        + [jax.ShapeDtypeStruct((width, size), bf16)] * (ways - 1),
        compiler_params=small_grant(4),
        name="split",
    )(digit[None], own, *parts)


def join_kernel(digit_ref, *refs):
    parts, out_ref = refs[:-1], refs[-1]
    size = parts[0].shape[1]
    for s, part in enumerate(reversed(parts)):
        rows = pl.ds(pl.multiple_of((digit_ref[0] ^ s) * size, size), size)
        out_ref[rows, :] = part[...].astype(f32).T


def join(digit, parts):
    width, size = parts[0].shape
    return pl.pallas_call(
        join_kernel,
        in_specs=[smem_spec()] + [vmem_spec()] * len(parts),
        out_specs=vmem_spec(),
        out_shape=jax.ShapeDtypeStruct((size * len(parts), width), f32),
        compiler_params=small_grant(4),
        name="join",
    )(digit[None], *parts)


def body(features, proj_weight, row_lse, positive):
    rows = features.shape[0]
    dp_count = lax.axis_size("dp")
    pair_count = lax.axis_size("pair")
    far = pair_count // 4
    group_rows = rows * dp_count
    block = lax.axis_index("pair").astype(jnp.int32)
    core = lax.axis_index("dp").astype(jnp.int32)

    lse_rows = row_lse.reshape(rows // lanes, lanes)
    positive_rows = positive.reshape(rows // lanes, lanes)
    projected, packed, held = project(features, proj_weight, lse_rows, positive_rows)

    def pairing(count, stride, odd):
        size = count // stride
        return lambda i: (((i // stride + odd) % size ^ 1) + size - odd) % size * stride + i % stride

    def partner(stride, odd, turn=1):
        to = pairing(pair_count, stride, odd)
        return crossed(packed, to, turn), to(block) * group_rows + (core ^ turn) * rows

    (near_even, base_a), (far_even, base_b) = partner(1, 0, 1), partner(far, 0, 1)
    (far_odd, base_c), (near_odd, base_d) = partner(far, 1, 0), partner(1, 1, 1)
    siblings = [swapped(packed, mask) for mask in range(1, dp_count)]
    owns = siblings + [packed]
    acc = couple([base_c], owns, [far_odd])
    acc = couple([base_a, base_b], owns, [near_even, far_even], (acc,))
    acc_siblings = couple([base_d], siblings, [near_odd], (acc,))
    returned = [swapped(acc_siblings[mask - 1], mask) for mask in range(1, dp_count)]
    acc = couple([base_d], [packed], [near_odd], (acc[dp_count - 1 :],))
    grad_embed, half, *sends = finish(core, acc, projected, held, returned, dp_count)
    received = [swapped(send, mask) for mask, send in enumerate(sends, 1)]
    mine = weight_term(half, held, core, dp_count)

    ways = 4
    digit = block & (ways - 1)
    keep, *sends = split(digit, mine, received, ways)
    moved = [exchanged(sends[s - 1], s) for s in (1, 2, 3)]
    for part in moved:
        keep = keep + part.astype(f32)
    stride = ways
    while stride < pair_count:
        mine = keep.astype(bf16)
        last, middle, near = (exchanged(mine, s * stride).astype(f32) for s in (3, 2, 1))
        keep = (last + near) + (middle + mine.astype(f32))
        stride *= ways
    mine = keep.astype(bf16)
    moved = [exchanged(mine, s) for s in reversed(range(1, ways))]
    return (grad_embed, join(digit, moved + [mine]))


def solution(mesh):
    return jax.shard_map(
        body,
        mesh=mesh,
        in_specs=(P(("pair", "dp"), None), P(), P(("pair", "dp")), P(("pair", "dp"))),
        out_specs=(P(("pair", "dp"), None), P("dp", None)),
        check_vma=False,
    )
```

```python
import functools
import math

import jax
import jax.numpy as jnp
from jax import lax
from jax.experimental import pallas as pl
from jax.experimental.pallas import tpu as pltpu
from jax.sharding import PartitionSpec as P

inverse_temperature = 10.0
exponent_scale = 10.0 * math.log2(math.e)
epsilon = 1e-06
lanes = 128
tail = 16
f32, bf16 = jnp.float32, jnp.bfloat16


def swapped(value, mask):
    count = lax.axis_size("dp")
    return lax.ppermute(value, "dp", [(d, d ^ mask) for d in range(count)])


def exchanged(value, mask):
    count = lax.axis_size("pair")
    return lax.ppermute(value, "pair", [(p, p ^ mask) for p in range(count)])


def crossed(value, to, turn=1):
    blocks, cores = lax.axis_size("pair"), lax.axis_size("dp")
    pairs = [
        (block * cores + core, to(block) * cores + (core ^ turn))
        for block in range(blocks)
        for core in range(cores)
    ]
    return lax.ppermute(value, ("pair", "dp"), pairs)


def vmem_spec():
    return pl.BlockSpec(memory_space=pltpu.VMEM)


def smem_spec():
    return pl.BlockSpec(memory_space=pltpu.SMEM)


def small_grant(mib):
    return pltpu.CompilerParams(vmem_limit_bytes=mib * 2**20)


def project_kernel(
    features_ref,
    weight_ref,
    lse_ref,
    positive_ref,
    projected_ref,
    packed_ref,
    held,
    weight,
    lse,
    positive,
    sems,
    small_sems,
):
    rows = held.shape[0]
    chunks = sems.shape[0]
    chunk = rows // chunks
    weight_copy = pltpu.make_async_copy(weight_ref, weight, small_sems.at[0])
    lse_copy = pltpu.make_async_copy(lse_ref, lse, small_sems.at[1])
    positive_copy = pltpu.make_async_copy(positive_ref, positive, small_sems.at[2])
    copies = []
    for k in range(chunks):
        part = pl.ds(k * chunk, chunk)
        copies.append(
            pltpu.make_async_copy(features_ref.at[part, :], held.at[part, :], sems.at[k])
        )
    for copy in [weight_copy] + copies + [lse_copy, positive_copy]:
        copy.start()
    weight_copy.wait()
    for k, copy in enumerate(copies):
        part = pl.ds(k * chunk, chunk)
        copy.wait()
        projected = jnp.dot(held[part, :], weight[...], preferred_element_type=f32)
        magnitude = jnp.sqrt(jnp.sum(projected * projected, axis=-1, keepdims=True) + epsilon)
        projected_ref[part, :] = projected
        packed_ref[part, :] = (projected / magnitude).astype(bf16)
    lse_copy.wait()
    positive_copy.wait()
    index = positive[...]
    packed_ref[pl.ds(rows, tail), :] = jnp.concatenate(
        [lse[...].astype(f32)]
        + [((index >> shift) & 127).astype(f32) for shift in (14, 7, 0)],
        axis=0,
    ).astype(bf16)


def project(features, weight, lse_rows, positive_rows):
    rows, units = features.shape
    width = weight.shape[1]
    chunks = 2
    hbm = pl.BlockSpec(memory_space=pltpu.HBM)
    return pl.pallas_call(
        project_kernel,
        in_specs=[hbm] * 4,
        out_specs=[vmem_spec()] * 3,
        out_shape=[
            jax.ShapeDtypeStruct((rows, width), f32),
            jax.ShapeDtypeStruct((rows + tail, width), bf16),
            jax.ShapeDtypeStruct((rows, units), bf16),
        ],
        scratch_shapes=[
            pltpu.VMEM((units, width), bf16),
            pltpu.VMEM(lse_rows.shape, lse_rows.dtype),
            pltpu.VMEM(positive_rows.shape, positive_rows.dtype),
            pltpu.SemaphoreType.DMA((chunks,)),
            pltpu.SemaphoreType.DMA((3,)),
        ],
        compiler_params=small_grant(8),
        name="project",
    )(
        *(
            pltpu.with_memory_space_constraint(value, pltpu.HBM)
            for value in (features, weight, lse_rows, positive_rows)
        )
    )


def as_columns(rows):
    return jnp.concatenate(
        [
            jnp.broadcast_to(rows[k : k + 1, :], (lanes, lanes)).T
            for k in range(rows.shape[0])
        ],
        axis=0,
    )


def coupled_rows(columns, bases, own_ref, parts, total):
    rows = own_ref.shape[0] - tail
    step = min(256, rows)
    column = lax.broadcasted_iota(jnp.int32, (1, lanes), 1)
    own = own_ref[pl.ds(0, rows), :]
    weight_i, positive_i = columns
    for which, part in enumerate(parts):
        part_weight = jnp.exp(-part[pl.ds(rows, tail), :].astype(f32))
        for begin in range(0, rows, step):
            other = part[pl.ds(begin, step), :]
            cosine = lax.dot_general(
                own, other, (((1,), (1,)), ((), ())), preferred_element_type=f32
            )
            pieces = []
            for lane in range(0, step, lanes):
                k = (begin + lane) // lanes
                grown = jnp.exp2(cosine[:, lane : lane + lanes] * exponent_scale)
                ids = (column + (bases[which][0] + (begin + lane))).astype(f32)
                value = grown * (weight_i + part_weight[k : k + 1, :])
                value = value - jnp.where(positive_i == ids, 2.0, 0.0)
                pieces.append(value.astype(bf16))
            coupling = jnp.concatenate(pieces, axis=1)
            total = total + jnp.dot(coupling, other, preferred_element_type=f32)
    return total


def own_columns(own_ref):
    rows = own_ref.shape[0] - tail
    count = rows // lanes
    values = own_ref[pl.ds(rows, tail), :].astype(f32)
    lse, high, middle, low = (values[k * count : (k + 1) * count, :] for k in range(4))
    positive = (high * 128.0 + middle) * 128.0 + low
    return as_columns(jnp.exp(-lse)), as_columns(positive)


def couple_kernel(owners, count, *refs):
    bases, refs = refs[:count], refs[count:]
    owns, parts, before, acc_ref = (
        refs[:owners], refs[owners : owners + count], refs[owners + count : -1], refs[-1]
    )
    rows = owns[0].shape[0] - tail
    for k, own_ref in enumerate(owns):
        columns = own_columns(own_ref)
        total = before[0][k] if before else jnp.zeros((rows, own_ref.shape[1]), f32)
        acc_ref[k] = coupled_rows(columns, bases, own_ref, parts, total)


def couple_cost(rows, width, count):
    pairs = rows * rows * count
    return pl.CostEstimate(
        flops=4 * pairs * width, bytes_accessed=rows * width * 4, transcendentals=pairs
    )


def couple(bases, owns, parts, before=()):
    rows, width = owns[0].shape[0] - tail, owns[0].shape[1]
    return pl.pallas_call(
        functools.partial(couple_kernel, len(owns), len(parts)),
        in_specs=[smem_spec()] * len(parts) + [vmem_spec()] * (len(owns) + len(parts) + len(before)),
        out_specs=vmem_spec(),
        out_shape=jax.ShapeDtypeStruct((len(owns), rows, width), f32),
        compiler_params=small_grant(8),
        cost_estimate=couple_cost(rows, width, len(parts) * len(owns)),
        name="couple",
    )(*(base[None] for base in bases), *owns, *parts, *before)


def finish_kernel(count, core_ref, acc_ref, projected_ref, features_ref, *refs):
    received, grad_ref, half_ref, sends = refs[:count], refs[count], refs[count + 1], refs[count + 2 :]
    rows = projected_ref.shape[0]
    chunk = min(128, rows)
    for start in range(0, rows, chunk):
        part = pl.ds(start, chunk)
        total = acc_ref[0, part, :]
        for other in received:
            total = total + other[part, :]
        projected = projected_ref[part, :]
        magnitude = jnp.sqrt(jnp.sum(projected * projected, axis=-1, keepdims=True) + epsilon)
        unit = projected / magnitude
        upstream = total * inverse_temperature
        grad = (upstream - unit * jnp.sum(unit * upstream, axis=-1, keepdims=True)) / magnitude
        grad_ref[part, :] = grad
        half_ref[:, part] = grad.T.astype(bf16)
    for mask, send in enumerate(sends, 1):
        weight_columns(half_ref, features_ref, core_ref[0] ^ mask, send)


def weight_columns(half_ref, features_ref, share, out_ref):
    size = out_ref.shape[1]
    chunk = min(256, size)
    for start in range(0, size, chunk):
        columns = pl.ds(pl.multiple_of(share * size + start, chunk), chunk)
        out_ref[:, pl.ds(start, chunk)] = jnp.dot(
            half_ref[...], features_ref[:, columns], preferred_element_type=f32
        ).astype(out_ref.dtype)


def finish(core, acc, projected, features, received, shares):
    rows, width = projected.shape
    units = features.shape[1]
    return pl.pallas_call(
        functools.partial(finish_kernel, len(received)),
        in_specs=[smem_spec()] + [vmem_spec()] * (3 + len(received)),
        out_specs=[vmem_spec()] * (1 + shares),
        out_shape=[
            pltpu.VMEM((rows, width), f32),
            jax.ShapeDtypeStruct((width, rows), bf16),
        ]
        + [jax.ShapeDtypeStruct((width, units // shares), bf16)] * (shares - 1),
        compiler_params=small_grant(8),
        name="finish",
    )(core[None], acc, projected, features, *received)


def weight_kernel(share_ref, half_ref, features_ref, out_ref):
    weight_columns(half_ref, features_ref, share_ref[0], out_ref)


def weight_term(half, features, share, shares):
    width, rows = half.shape
    size = features.shape[1] // shares
    return pl.pallas_call(
        weight_kernel,
        in_specs=[smem_spec()] + [vmem_spec()] * 2,
        out_specs=vmem_spec(),
        out_shape=jax.ShapeDtypeStruct((width, size), f32),
        compiler_params=small_grant(8),
        cost_estimate=pl.CostEstimate(
            flops=2 * rows * size * width, bytes_accessed=rows * size * 2, transcendentals=0
        ),
        name="weight_term",
    )(share[None], half, features)


def split_kernel(count, digit_ref, own_ref, *refs):
    parts, keep_ref, sends = refs[:count], refs[count], refs[count + 1 :]
    size = keep_ref.shape[1]
    for s in range(len(sends) + 1):
        columns = pl.ds(pl.multiple_of((digit_ref[0] ^ s) * size, size), size)
        total = own_ref[:, columns]
        for part in parts:
            total = total + part[:, columns].astype(f32)
        if s == 0:
            keep_ref[...] = total
        else:
            sends[s - 1][...] = total.astype(bf16)


def split(digit, own, parts, ways):
    width, size = own.shape[0], own.shape[1] // ways
    return pl.pallas_call(
        functools.partial(split_kernel, len(parts)),
        in_specs=[smem_spec()] + [vmem_spec()] * (1 + len(parts)),
        out_specs=[vmem_spec()] * ways,
        out_shape=[jax.ShapeDtypeStruct((width, size), f32)]
        + [jax.ShapeDtypeStruct((width, size), bf16)] * (ways - 1),
        compiler_params=small_grant(4),
        name="split",
    )(digit[None], own, *parts)


def join_kernel(digit_ref, *refs):
    parts, out_ref = refs[:-1], refs[-1]
    size = parts[0].shape[1]
    for s, part in enumerate(reversed(parts)):
        rows = pl.ds(pl.multiple_of((digit_ref[0] ^ s) * size, size), size)
        out_ref[rows, :] = part[...].astype(f32).T


def join(digit, parts):
    width, size = parts[0].shape
    return pl.pallas_call(
        join_kernel,
        in_specs=[smem_spec()] + [vmem_spec()] * len(parts),
        out_specs=vmem_spec(),
        out_shape=jax.ShapeDtypeStruct((size * len(parts), width), f32),
        compiler_params=small_grant(4),
        name="join",
    )(digit[None], *parts)


def body(features, proj_weight, row_lse, positive):
    rows = features.shape[0]
    dp_count = lax.axis_size("dp")
    pair_count = lax.axis_size("pair")
    far = pair_count // 4
    group_rows = rows * dp_count
    block = lax.axis_index("pair").astype(jnp.int32)
    core = lax.axis_index("dp").astype(jnp.int32)

    lse_rows = row_lse.reshape(rows // lanes, lanes)
    positive_rows = positive.reshape(rows // lanes, lanes)
    projected, packed, held = project(features, proj_weight, lse_rows, positive_rows)

    def pairing(count, stride, odd):
        size = count // stride
        return lambda i: (((i // stride + odd) % size ^ 1) + size - odd) % size * stride + i % stride

    def partner(stride, odd, turn=1):
        to = pairing(pair_count, stride, odd)
        return crossed(packed, to, turn), to(block) * group_rows + (core ^ turn) * rows

    (near_even, base_a), (far_even, base_b) = partner(1, 0, 1), partner(far, 0, 1)
    (far_odd, base_c), (near_odd, base_d) = partner(far, 1, 0), partner(1, 1, 1)
    siblings = [swapped(packed, mask) for mask in range(1, dp_count)]
    owns = siblings + [packed]
    acc = couple([base_c], owns, [far_odd])
    acc = couple([base_d], owns, [near_odd], (acc,))
    acc_siblings = couple([base_a, base_b], siblings, [near_even, far_even], (acc,))
    returned = [swapped(acc_siblings[mask - 1], mask) for mask in range(1, dp_count)]
    acc = couple([base_a, base_b], [packed], [near_even, far_even], (acc[dp_count - 1 :],))
    grad_embed, half, *sends = finish(core, acc, projected, held, returned, dp_count)
    received = [swapped(send, mask) for mask, send in enumerate(sends, 1)]
    mine = weight_term(half, held, core, dp_count)

    ways = 4
    digit = block & (ways - 1)
    keep, *sends = split(digit, mine, received, ways)
    moved = [exchanged(sends[s - 1], s) for s in (1, 2, 3)]
    for part in moved:
        keep = keep + part.astype(f32)
    stride = ways
    while stride < pair_count:
        mine = keep.astype(bf16)
        last, middle, near = (exchanged(mine, s * stride).astype(f32) for s in (3, 2, 1))
        keep = (last + near) + (middle + mine.astype(f32))
        stride *= ways
    mine = keep.astype(bf16)
    moved = [exchanged(mine, s) for s in reversed(range(1, ways))]
    return (grad_embed, join(digit, moved + [mine]))


def solution(mesh):
    return jax.shard_map(
        body,
        mesh=mesh,
        in_specs=(P(("pair", "dp"), None), P(), P(("pair", "dp")), P(("pair", "dp"))),
        out_specs=(P(("pair", "dp"), None), P("dp", None)),
        check_vma=False,
    )
```

```python
import functools
import math

import jax
import jax.numpy as jnp
from jax import lax
from jax.experimental import pallas as pl
from jax.experimental.pallas import tpu as pltpu
from jax.sharding import PartitionSpec as P

inverse_temperature = 10.0
exponent_scale = 10.0 * math.log2(math.e)
epsilon = 1e-06
lanes = 128
tail = 16
f32, bf16 = jnp.float32, jnp.bfloat16


def swapped(value, mask):
    count = lax.axis_size("dp")
    return lax.ppermute(value, "dp", [(d, d ^ mask) for d in range(count)])


def exchanged(value, mask):
    count = lax.axis_size("pair")
    return lax.ppermute(value, "pair", [(p, p ^ mask) for p in range(count)])


def crossed(value, to, turn=1):
    blocks, cores = lax.axis_size("pair"), lax.axis_size("dp")
    pairs = [
        (block * cores + core, to(block) * cores + (core ^ turn))
        for block in range(blocks)
        for core in range(cores)
    ]
    return lax.ppermute(value, ("pair", "dp"), pairs)


def vmem_spec():
    return pl.BlockSpec(memory_space=pltpu.VMEM)


def smem_spec():
    return pl.BlockSpec(memory_space=pltpu.SMEM)


def small_grant(mib):
    return pltpu.CompilerParams(vmem_limit_bytes=mib * 2**20)


def project_kernel(
    features_ref,
    weight_ref,
    lse_ref,
    positive_ref,
    projected_ref,
    packed_ref,
    held,
    weight,
    lse,
    positive,
    sems,
    small_sems,
):
    rows = held.shape[0]
    chunks = sems.shape[0]
    chunk = rows // chunks
    weight_copy = pltpu.make_async_copy(weight_ref, weight, small_sems.at[0])
    lse_copy = pltpu.make_async_copy(lse_ref, lse, small_sems.at[1])
    positive_copy = pltpu.make_async_copy(positive_ref, positive, small_sems.at[2])
    copies = []
    for k in range(chunks):
        part = pl.ds(k * chunk, chunk)
        copies.append(
            pltpu.make_async_copy(features_ref.at[part, :], held.at[part, :], sems.at[k])
        )
    for copy in [weight_copy] + copies + [lse_copy, positive_copy]:
        copy.start()
    weight_copy.wait()
    for k, copy in enumerate(copies):
        part = pl.ds(k * chunk, chunk)
        copy.wait()
        projected = jnp.dot(held[part, :], weight[...], preferred_element_type=f32)
        magnitude = jnp.sqrt(jnp.sum(projected * projected, axis=-1, keepdims=True) + epsilon)
        projected_ref[part, :] = projected
        packed_ref[part, :] = (projected / magnitude).astype(bf16)
    lse_copy.wait()
    positive_copy.wait()
    index = positive[...]
    packed_ref[pl.ds(rows, tail), :] = jnp.concatenate(
        [lse[...].astype(f32)]
        + [((index >> shift) & 127).astype(f32) for shift in (14, 7, 0)],
        axis=0,
    ).astype(bf16)


def project(features, weight, lse_rows, positive_rows):
    rows, units = features.shape
    width = weight.shape[1]
    chunks = 2
    hbm = pl.BlockSpec(memory_space=pltpu.HBM)
    return pl.pallas_call(
        project_kernel,
        in_specs=[hbm] * 4,
        out_specs=[vmem_spec()] * 3,
        out_shape=[
            jax.ShapeDtypeStruct((rows, width), f32),
            jax.ShapeDtypeStruct((rows + tail, width), bf16),
            jax.ShapeDtypeStruct((rows, units), bf16),
        ],
        scratch_shapes=[
            pltpu.VMEM((units, width), bf16),
            pltpu.VMEM(lse_rows.shape, lse_rows.dtype),
            pltpu.VMEM(positive_rows.shape, positive_rows.dtype),
            pltpu.SemaphoreType.DMA((chunks,)),
            pltpu.SemaphoreType.DMA((3,)),
        ],
        compiler_params=small_grant(8),
        name="project",
    )(
        *(
            pltpu.with_memory_space_constraint(value, pltpu.HBM)
            for value in (features, weight, lse_rows, positive_rows)
        )
    )


def as_columns(rows):
    return jnp.concatenate(
        [
            jnp.broadcast_to(rows[k : k + 1, :], (lanes, lanes)).T
            for k in range(rows.shape[0])
        ],
        axis=0,
    )


def coupled_rows(columns, bases, own_ref, parts, total):
    rows = own_ref.shape[0] - tail
    step = min(256, rows)
    column = lax.broadcasted_iota(jnp.int32, (1, lanes), 1)
    own = own_ref[pl.ds(0, rows), :]
    weight_i, positive_i = columns
    for which, part in enumerate(parts):
        part_weight = jnp.exp(-part[pl.ds(rows, tail), :].astype(f32))
        for begin in range(0, rows, step):
            other = part[pl.ds(begin, step), :]
            cosine = lax.dot_general(
                own, other, (((1,), (1,)), ((), ())), preferred_element_type=f32
            )
            pieces = []
            for lane in range(0, step, lanes):
                k = (begin + lane) // lanes
                grown = jnp.exp2(cosine[:, lane : lane + lanes] * exponent_scale)
                ids = (column + (bases[which][0] + (begin + lane))).astype(f32)
                value = grown * (weight_i + part_weight[k : k + 1, :])
                value = value - jnp.where(positive_i == ids, 2.0, 0.0)
                pieces.append(value.astype(bf16))
            coupling = jnp.concatenate(pieces, axis=1)
            total = total + jnp.dot(coupling, other, preferred_element_type=f32)
    return total


def own_columns(own_ref):
    rows = own_ref.shape[0] - tail
    count = rows // lanes
    values = own_ref[pl.ds(rows, tail), :].astype(f32)
    lse, high, middle, low = (values[k * count : (k + 1) * count, :] for k in range(4))
    positive = (high * 128.0 + middle) * 128.0 + low
    return as_columns(jnp.exp(-lse)), as_columns(positive)


def couple_kernel(owners, count, *refs):
    bases, refs = refs[:count], refs[count:]
    owns, parts, before, acc_ref = (
        refs[:owners], refs[owners : owners + count], refs[owners + count : -1], refs[-1]
    )
    rows = owns[0].shape[0] - tail
    for k, own_ref in enumerate(owns):
        columns = own_columns(own_ref)
        total = before[0][k] if before else jnp.zeros((rows, own_ref.shape[1]), f32)
        acc_ref[k] = coupled_rows(columns, bases, own_ref, parts, total)


def couple_cost(rows, width, count):
    pairs = rows * rows * count
    return pl.CostEstimate(
        flops=4 * pairs * width, bytes_accessed=rows * width * 4, transcendentals=pairs
    )


def couple(bases, owns, parts, before=()):
    rows, width = owns[0].shape[0] - tail, owns[0].shape[1]
    return pl.pallas_call(
        functools.partial(couple_kernel, len(owns), len(parts)),
        in_specs=[smem_spec()] * len(parts) + [vmem_spec()] * (len(owns) + len(parts) + len(before)),
        out_specs=vmem_spec(),
        out_shape=jax.ShapeDtypeStruct((len(owns), rows, width), f32),
        compiler_params=small_grant(8),
        cost_estimate=couple_cost(rows, width, len(parts) * len(owns)),
        name="couple",
    )(*(base[None] for base in bases), *owns, *parts, *before)


def finish_kernel(count, core_ref, acc_ref, projected_ref, features_ref, *refs):
    received, grad_ref, half_ref, sends = refs[:count], refs[count], refs[count + 1], refs[count + 2 :]
    rows = projected_ref.shape[0]
    chunk = min(128, rows)
    for start in range(0, rows, chunk):
        part = pl.ds(start, chunk)
        total = acc_ref[0, part, :]
        for other in received:
            total = total + other[part, :]
        projected = projected_ref[part, :]
        magnitude = jnp.sqrt(jnp.sum(projected * projected, axis=-1, keepdims=True) + epsilon)
        unit = projected / magnitude
        upstream = total * inverse_temperature
        grad = (upstream - unit * jnp.sum(unit * upstream, axis=-1, keepdims=True)) / magnitude
        grad_ref[part, :] = grad
        half_ref[:, part] = grad.T.astype(bf16)
    for mask, send in enumerate(sends, 1):
        weight_columns(half_ref, features_ref, core_ref[0] ^ mask, send)


def weight_columns(half_ref, features_ref, share, out_ref):
    size = out_ref.shape[1]
    chunk = min(256, size)
    for start in range(0, size, chunk):
        columns = pl.ds(pl.multiple_of(share * size + start, chunk), chunk)
        out_ref[:, pl.ds(start, chunk)] = jnp.dot(
            half_ref[...], features_ref[:, columns], preferred_element_type=f32
        ).astype(out_ref.dtype)


def finish(core, acc, projected, features, received, shares):
    rows, width = projected.shape
    units = features.shape[1]
    return pl.pallas_call(
        functools.partial(finish_kernel, len(received)),
        in_specs=[smem_spec()] + [vmem_spec()] * (3 + len(received)),
        out_specs=[vmem_spec()] * (1 + shares),
        out_shape=[
            pltpu.VMEM((rows, width), f32),
            jax.ShapeDtypeStruct((width, rows), bf16),
        ]
        + [jax.ShapeDtypeStruct((width, units // shares), bf16)] * (shares - 1),
        compiler_params=small_grant(8),
        name="finish",
    )(core[None], acc, projected, features, *received)


def weight_kernel(share_ref, half_ref, features_ref, out_ref):
    weight_columns(half_ref, features_ref, share_ref[0], out_ref)


def weight_term(half, features, share, shares):
    width, rows = half.shape
    size = features.shape[1] // shares
    return pl.pallas_call(
        weight_kernel,
        in_specs=[smem_spec()] + [vmem_spec()] * 2,
        out_specs=vmem_spec(),
        out_shape=jax.ShapeDtypeStruct((width, size), f32),
        compiler_params=small_grant(8),
        cost_estimate=pl.CostEstimate(
            flops=2 * rows * size * width, bytes_accessed=rows * size * 2, transcendentals=0
        ),
        name="weight_term",
    )(share[None], half, features)


def split_kernel(count, digit_ref, own_ref, *refs):
    parts, keep_ref, sends = refs[:count], refs[count], refs[count + 1 :]
    size = keep_ref.shape[1]
    for s in range(len(sends) + 1):
        columns = pl.ds(pl.multiple_of((digit_ref[0] ^ s) * size, size), size)
        total = own_ref[:, columns]
        for part in parts:
            total = total + part[:, columns].astype(f32)
        if s == 0:
            keep_ref[...] = total
        else:
            sends[s - 1][...] = total.astype(bf16)


def split(digit, own, parts, ways):
    width, size = own.shape[0], own.shape[1] // ways
    return pl.pallas_call(
        functools.partial(split_kernel, len(parts)),
        in_specs=[smem_spec()] + [vmem_spec()] * (1 + len(parts)),
        out_specs=[vmem_spec()] * ways,
        out_shape=[jax.ShapeDtypeStruct((width, size), f32)]
        + [jax.ShapeDtypeStruct((width, size), bf16)] * (ways - 1),
        compiler_params=small_grant(4),
        name="split",
    )(digit[None], own, *parts)


def join_kernel(digit_ref, *refs):
    parts, out_ref = refs[:-1], refs[-1]
    size = parts[0].shape[1]
    for s, part in enumerate(reversed(parts)):
        rows = pl.ds(pl.multiple_of((digit_ref[0] ^ s) * size, size), size)
        out_ref[rows, :] = part[...].astype(f32).T


def join(digit, parts):
    width, size = parts[0].shape
    return pl.pallas_call(
        join_kernel,
        in_specs=[smem_spec()] + [vmem_spec()] * len(parts),
        out_specs=vmem_spec(),
        out_shape=jax.ShapeDtypeStruct((size * len(parts), width), f32),
        compiler_params=small_grant(4),
        name="join",
    )(digit[None], *parts)


def body(features, proj_weight, row_lse, positive):
    rows = features.shape[0]
    dp_count = lax.axis_size("dp")
    pair_count = lax.axis_size("pair")
    far = pair_count // 4
    group_rows = rows * dp_count
    block = lax.axis_index("pair").astype(jnp.int32)
    core = lax.axis_index("dp").astype(jnp.int32)

    lse_rows = row_lse.reshape(rows // lanes, lanes)
    positive_rows = positive.reshape(rows // lanes, lanes)
    projected, packed, held = project(features, proj_weight, lse_rows, positive_rows)

    def pairing(count, stride, odd):
        size = count // stride
        return lambda i: (((i // stride + odd) % size ^ 1) + size - odd) % size * stride + i % stride

    def partner(stride, odd, turn=1):
        to = pairing(pair_count, stride, odd)
        return crossed(packed, to, turn), to(block) * group_rows + (core ^ turn) * rows

    (near_even, base_a), (far_even, base_b) = partner(1, 0, 1), partner(far, 0, 1)
    (far_odd, base_c), (near_odd, base_d) = partner(far, 1, 0), partner(1, 1, 1)
    siblings = [swapped(packed, mask) for mask in range(1, dp_count)]
    owns = siblings + [packed]
    acc = couple([base_c], owns, [far_odd])
    acc = couple([base_d], owns, [near_odd], (acc,))
    acc_siblings = couple([base_b, base_a], siblings, [far_even, near_even], (acc,))
    returned = [swapped(acc_siblings[mask - 1], mask) for mask in range(1, dp_count)]
    acc = couple([base_b, base_a], [packed], [far_even, near_even], (acc[dp_count - 1 :],))
    grad_embed, half, *sends = finish(core, acc, projected, held, returned, dp_count)
    received = [swapped(send, mask) for mask, send in enumerate(sends, 1)]
    mine = weight_term(half, held, core, dp_count)

    ways = 4
    digit = block & (ways - 1)
    keep, *sends = split(digit, mine, received, ways)
    moved = [exchanged(sends[s - 1], s) for s in (1, 2, 3)]
    for part in moved:
        keep = keep + part.astype(f32)
    stride = ways
    while stride < pair_count:
        mine = keep.astype(bf16)
        last, middle, near = (exchanged(mine, s * stride).astype(f32) for s in (3, 2, 1))
        keep = (last + near) + (middle + mine.astype(f32))
        stride *= ways
    mine = keep.astype(bf16)
    moved = [exchanged(mine, s) for s in reversed(range(1, ways))]
    return (grad_embed, join(digit, moved + [mine]))


def solution(mesh):
    return jax.shard_map(
        body,
        mesh=mesh,
        in_specs=(P(("pair", "dp"), None), P(), P(("pair", "dp")), P(("pair", "dp"))),
        out_specs=(P(("pair", "dp"), None), P("dp", None)),
        check_vma=False,
    )
```
